128 devices in a mesh: swath: 4 (over z), col: 32 (over x, y, core).
Axes of the slice: x: 4, y: 4, z: 4, core: 2. Of those that a mesh axis runs over, the one named last changes fastest.
Arguments:
- raw_band: float32 [4096, 32768], P('swath', 'col'), may hold values from -6 to 6
- section_offsets: int32 [32, 2], replicated, may hold values from -16 to 16, as said below
Outputs:
- diffused: float32 [4096, 32768], P('swath', 'col')
- defect: float32 [4096, 32768], P('swath', 'col')
The draws below stay inside these ranges and needn't reach their ends.
Inputs may be any that keep to these rules, and one draw needn't show every extreme that they name: `section_offsets`: row and column shifts of each die; some die has each extreme in each of the two columns.
All inputs are finite; a program needn't handle non-finite values.
Results may differ from the reference program's by a relative error of at most 0.0003.
Values sent between devices are 32-bit elements; how exact they have to be, the bound alone decides.
A program may use at most 128 MiB of HBM per device.

```python
import jax
import jax.numpy as jnp
from jax import lax

STEPS = 4
MAXOFF = 16
DIES = 32
NR = 4096
NC = 32768
N_COL = 32


def draw_section_offsets(key, part):
    first_key, second_key, third_key = jax.random.split(jax.random.fold_in(key, 11), 3)
    base_offsets = jax.random.randint(first_key, (DIES, 2), -MAXOFF, MAXOFF + 1)
    first_die = jax.random.randint(second_key, (2,), 0, DIES)
    step_dies = jax.random.randint(third_key, (2,), 1, DIES)
    second_die = (first_die + step_dies) % DIES
    die_ids = jnp.arange(DIES)[:, None]
    base_offsets = jnp.where(die_ids == first_die[None, :], MAXOFF, base_offsets)
    base_offsets = jnp.where(die_ids == second_die[None, :], -MAXOFF, base_offsets)
    return base_offsets.astype(jnp.int32)


def levels(own_key, dims, shards, least, top_value):
    loudness, own = 1.0, jax.random.fold_in(own_key, 6)
    for position, blocks in shards:
        heights = jnp.exp(jax.random.uniform(jax.random.fold_in(own, position), (blocks,), jnp.float32, least / len(shards), top_value / len(shards)))
        loudness = loudness * jnp.repeat(heights, dims[position] // blocks).reshape([-1 if axis == position else 1 for axis in range(len(dims))])
    return loudness


def bell_draw(stream_key, extent, deviation, bound, shards=(), kind=jnp.bfloat16):
    entries = jax.random.normal(stream_key, extent, jnp.float32) * deviation
    if len(shards) > 0:
        entries = levels(stream_key, extent, shards, -0.22, 0.18) * entries
    return jnp.clip(entries, min=-bound, max=bound).astype(kind)


def setup_inputs(seed: int = 0) -> dict:
    streams_of = jax.random.split(jax.random.key(seed), 3)
    return {
        "raw_band": bell_draw(streams_of[0], (NR, NC), 1.0, 6.0, ((0, 4), (1, 32)), jnp.float32),
        "section_offsets": draw_section_offsets(jax.random.fold_in(streams_of[2], 71), 0),
    }


step_rate = 0.2


def conduct_flux(middle, beside):
    differ = beside - middle
    return differ / (1.0 + differ * differ)


def diffuse_inner(bordered):
    middle = bordered[1:-1, 1:-1]
    flux_sum = conduct_flux(middle, bordered[:-2, 1:-1]) + conduct_flux(middle, bordered[2:, 1:-1])
    flux_sum = flux_sum + conduct_flux(middle, bordered[1:-1, :-2]) + conduct_flux(middle, bordered[1:-1, 2:])
    return middle + step_rate * flux_sum


def three_die(aligned, left_block, right_block):
    first_diff = aligned - left_block
    second_diff = aligned - right_block
    return jnp.maximum(jnp.minimum(first_diff, second_diff), 0.0) + jnp.minimum(jnp.maximum(first_diff, second_diff), 0.0)


def reference(raw_band, section_offsets):
    row_total, col_total = raw_band.shape
    die_count = N_COL
    die_width = col_total // die_count
    piece_width = die_width // die_count
    band = raw_band.reshape(row_total, die_count, die_count, piece_width).transpose(0, 2, 1, 3).reshape(row_total, col_total)
    current = band
    for step_index in range(STEPS):
        current = diffuse_inner(jnp.pad(current, 1, mode="edge"))
    padded = jnp.pad(current, MAXOFF)

    def align(die_index):
        start_row = (MAXOFF + section_offsets[die_index, 0]).astype(jnp.int32)
        start_col = (MAXOFF + die_index * die_width + section_offsets[die_index, 1]).astype(jnp.int32)
        return lax.dynamic_slice(padded, (start_row, start_col), (row_total, die_width))

    aligned = lax.map(align, jnp.arange(die_count, dtype=jnp.int32))
    defect = three_die(aligned, jnp.roll(aligned, 1, axis=0), jnp.roll(aligned, -1, axis=0))
    defect = defect.transpose(1, 0, 2).reshape(row_total, col_total)
    return current, defect
```

```python
import functools

import jax
import jax.numpy as jnp
from jax import lax
from jax.experimental import pallas as pl
from jax.experimental.pallas import tpu as pltpu
from jax.sharding import PartitionSpec as P

STEPS = 4
MAXOFF = 16
ROWH = 24
COLH = 64
PAD = 8
BLK = 8
step_rate = 0.2


def conduct_flux(differ):
    return differ / (1.0 + differ * differ)


def smooth_kernel(band_rows, band_cols, prm, tile, top, bot, side, diff_out, align_out, a_buf, b_buf, fv_buf):
    rows, width = tile.shape
    ext_w = a_buf.shape[1]
    ext_r = rows + 2 * ROWH
    row_base = prm[0] - ROWH
    col_base = prm[1]
    shift_r = prm[2]
    shift_c = prm[3]
    zeros_pad = jnp.zeros((PAD, ext_w), jnp.float32)
    for buf in (a_buf, b_buf, fv_buf):
        buf[pl.ds(0, PAD), :] = zeros_pad
        buf[pl.ds(PAD + ext_r, PAD), :] = zeros_pad
    a_buf[pl.ds(PAD, ROWH), pl.ds(0, width)] = top[...]
    a_buf[pl.ds(PAD + ROWH, rows), pl.ds(0, width)] = tile[...]
    a_buf[pl.ds(PAD + ROWH + rows, ROWH), pl.ds(0, width)] = bot[...]
    a_buf[pl.ds(PAD, ext_r), pl.ds(width, 2 * COLH)] = side[...]

    lane = lax.broadcasted_iota(jnp.int32, (BLK, ext_w), 1)
    gcol = col_base + lane - jnp.where(lane >= width + COLH, ext_w, 0)
    col_edge = (gcol >= 0) & (gcol <= band_cols - 2)
    sub = lax.broadcasted_iota(jnp.int32, (BLK, ext_w), 0)

    def step(src, dst):
        def body(i, carry):
            r0 = pl.multiple_of(PAD + i * BLK, BLK)
            pair = src[pl.ds(r0, 2 * BLK), :]
            here = pair[:BLK]
            below = pltpu.roll(pair, 2 * BLK - 1, 0)[:BLK]
            grow = row_base + (r0 - PAD) + sub
            row_edge = (grow >= 0) & (grow <= band_rows - 2)
            down = jnp.where(row_edge, conduct_flux(below - here), 0.0)
            fv_buf[pl.ds(r0, BLK), :] = down
            up = pltpu.roll(fv_buf[pl.ds(r0 - BLK, 2 * BLK), :], 1, 0)[BLK:]
            right = pltpu.roll(here, ext_w - 1, 1)
            across = jnp.where(col_edge, conduct_flux(right - here), 0.0)
            left = pltpu.roll(across, 1, 1)
            dst[pl.ds(r0, BLK), :] = here + step_rate * ((down - up) + (across - left))
            return carry
        lax.fori_loop(0, ext_r // BLK, body, 0)

    for k in range(STEPS):
        if k % 2 == 0:
            step(a_buf, b_buf)
        else:
            step(b_buf, a_buf)
    final = a_buf if STEPS % 2 == 0 else b_buf

    diff_out[...] = final[pl.ds(PAD + ROWH, rows), pl.ds(0, width)]

    roll_by = lax.rem(ext_w - shift_c, ext_w)
    gcol_a = col_base + shift_c + lax.broadcasted_iota(jnp.int32, (BLK, width), 1)
    col_in = (gcol_a >= 0) & (gcol_a < band_cols)
    sub_a = lax.broadcasted_iota(jnp.int32, (BLK, width), 0)

    start = PAD + ROWH + shift_r
    start_low = (start // BLK) * BLK
    row_roll = lax.rem(2 * BLK - (start - start_low), 2 * BLK)

    def emit(i, carry):
        r0 = pl.multiple_of(i * BLK, BLK)
        block = final[pl.ds(pl.multiple_of(start_low + r0, BLK), 2 * BLK), :]
        block = pltpu.roll(block, row_roll, 0)[:BLK]
        block = pltpu.roll(block, roll_by, 1)[:, :width]
        grow = prm[0] + shift_r + r0 + sub_a
        keep = col_in & (grow >= 0) & (grow < band_rows)
        align_out[pl.ds(r0, BLK), :] = jnp.where(keep, block, 0.0)
        return carry
    lax.fori_loop(0, rows // BLK, emit, 0)


def smooth(prm, tile, top, bot, side, band_rows, band_cols):
    rows, width = tile.shape
    ext_w = width + 2 * COLH
    buf = pltpu.VMEM((rows + 2 * ROWH + 2 * PAD, ext_w), jnp.float32)
    vspec = pl.BlockSpec(memory_space=pltpu.VMEM)
    return pl.pallas_call(
        functools.partial(smooth_kernel, band_rows, band_cols),
        out_shape=(jax.ShapeDtypeStruct((rows, width), jnp.float32),) * 2,
        in_specs=[pl.BlockSpec(memory_space=pltpu.SMEM)] + [vspec] * 4,
        out_specs=(vspec, vspec),
        scratch_shapes=[buf, buf, buf],
        compiler_params=pltpu.CompilerParams(vmem_limit_bytes=60 * 1024 * 1024),
        cost_estimate=pl.CostEstimate(flops=STEPS * 40 * (rows + 2 * ROWH) * ext_w, bytes_accessed=4 * 3 * rows * width, transcendentals=0),
    )(prm, tile, top, bot, side)


def from_behind(block, axis, distance):
    devices = range(lax.axis_size(axis))
    route = [((i - distance) % len(devices), i) for i in devices]
    return lax.ppermute(block, axis, route)


def from_grid(block, d_swath, d_col):
    swaths, cols = lax.axis_size("swath"), lax.axis_size("col")
    route = []
    for s in range(swaths):
        for c in range(cols):
            t, u = s + d_swath, c + d_col
            if 0 <= t < swaths and 0 <= u < cols:
                route.append((s * cols + c, t * cols + u))
    return lax.ppermute(block, ("swath", "col"), route)


def three_die(aligned, left_block, right_block):
    first_diff = aligned - left_block
    second_diff = aligned - right_block
    return jnp.maximum(jnp.minimum(first_diff, second_diff), 0.0) + jnp.minimum(
        jnp.maximum(first_diff, second_diff), 0.0
    )


def local(raw_band, section_offsets):
    col_count = lax.axis_size("col")
    swath_count = lax.axis_size("swath")
    row_total, die_width = raw_band.shape
    die_tile = lax.all_to_all(raw_band, "col", split_axis=1, concat_axis=1, tiled=True)
    swath_index = lax.axis_index("swath")
    col_index = lax.axis_index("col")
    band_rows = swath_count * row_total
    band_cols = col_count * die_width
    first_rows, last_rows = die_tile[:ROWH], die_tile[-ROWH:]
    first_cols, last_cols = die_tile[:, :COLH], die_tile[:, -COLH:]
    top = from_grid(last_rows, 1, 0)
    bot = from_grid(first_rows, -1, 0)
    right = jnp.concatenate(
        [from_grid(last_rows[:, :COLH], 1, -1), from_grid(first_cols, 0, -1), from_grid(first_rows[:, :COLH], -1, -1)], 0
    )
    left = jnp.concatenate(
        [from_grid(last_rows[:, -COLH:], 1, 1), from_grid(last_cols, 0, 1), from_grid(first_rows[:, -COLH:], -1, 1)], 0
    )
    side = jnp.concatenate([right, left], 1)
    die_ids = lax.broadcasted_iota(jnp.int32, section_offsets.shape, 0)
    own_shift = jnp.sum(jnp.where(die_ids == col_index, section_offsets, 0), axis=0)
    prm = jnp.stack(
        [swath_index * row_total, col_index * die_width, own_shift[0], own_shift[1]]
        + [jnp.int32(0)] * 4
    ).astype(jnp.int32)
    diffused, aligned = smooth(prm, die_tile, top, bot, side, band_rows, band_cols)
    left_block = from_behind(aligned, "col", 1)
    right_block = from_behind(aligned, "col", -1)
    defect = three_die(aligned, left_block, right_block)
    return (diffused, defect)


def solution(mesh):
    in_specs = (P("swath", "col"), P())
    out_specs = (P("swath", "col"), P("swath", "col"))
    return jax.shard_map(local, mesh=mesh, in_specs=in_specs, out_specs=out_specs, check_vma=False)
```

```python
import functools

import jax
import jax.numpy as jnp
from jax import lax
from jax.experimental import pallas as pl
from jax.experimental.pallas import tpu as pltpu
from jax.sharding import PartitionSpec as P

STEPS = 4
MAXOFF = 16
ROWH = 32
COLH = 64
PAD = 64
BLK = 64
step_rate = 0.2


def conduct_flux(differ):
    return differ / (1.0 + differ * differ)


def smooth_kernel(band_rows, band_cols, prm, tile, top, bot, side, diff_out, align_out, a_buf, b_buf, fv_buf):
    rows, width = tile.shape
    ext_w = a_buf.shape[1]
    ext_r = rows + 2 * ROWH
    row_base = prm[0] - ROWH
    col_base = prm[1]
    shift_r = prm[2]
    shift_c = prm[3]
    zeros_pad = jnp.zeros((PAD, ext_w), jnp.float32)
    for buf in (a_buf, b_buf, fv_buf):
        buf[pl.ds(0, PAD), :] = zeros_pad
        buf[pl.ds(PAD + ext_r, PAD), :] = zeros_pad
    a_buf[pl.ds(PAD, ROWH), pl.ds(0, width)] = top[...]
    a_buf[pl.ds(PAD + ROWH, rows), pl.ds(0, width)] = tile[...]
    a_buf[pl.ds(PAD + ROWH + rows, ROWH), pl.ds(0, width)] = bot[...]
    a_buf[pl.ds(PAD, ext_r), pl.ds(width, 2 * COLH)] = side[...]

    lane = lax.broadcasted_iota(jnp.int32, (BLK, ext_w), 1)
    gcol = col_base + lane - jnp.where(lane >= width + COLH, ext_w, 0)
    col_edge = (gcol >= 0) & (gcol <= band_cols - 2)
    sub = lax.broadcasted_iota(jnp.int32, (BLK, ext_w), 0)

    def step(src, dst):
        def body(i, carry):
            r0 = pl.multiple_of(PAD + i * BLK, BLK)
            pair = src[pl.ds(r0, 2 * BLK), :]
            here = pair[:BLK]
            below = pltpu.roll(pair, 2 * BLK - 1, 0)[:BLK]
            grow = row_base + (r0 - PAD) + sub
            row_edge = (grow >= 0) & (grow <= band_rows - 2)
            down = jnp.where(row_edge, conduct_flux(below - here), 0.0)
            fv_buf[pl.ds(r0, BLK), :] = down
            up = pltpu.roll(fv_buf[pl.ds(r0 - BLK, 2 * BLK), :], 1, 0)[BLK:]
            right = pltpu.roll(here, ext_w - 1, 1)
            across = jnp.where(col_edge, conduct_flux(right - here), 0.0)
            left = pltpu.roll(across, 1, 1)
            dst[pl.ds(r0, BLK), :] = here + step_rate * ((down - up) + (across - left))
            return carry
        lax.fori_loop(0, ext_r // BLK, body, 0)

    for k in range(STEPS):
        if k % 2 == 0:
            step(a_buf, b_buf)
        else:
            step(b_buf, a_buf)
    final = a_buf if STEPS % 2 == 0 else b_buf

    diff_out[...] = final[pl.ds(PAD + ROWH, rows), pl.ds(0, width)]

    roll_by = lax.rem(ext_w - shift_c, ext_w)
    gcol_a = col_base + shift_c + lax.broadcasted_iota(jnp.int32, (BLK, width), 1)
    col_in = (gcol_a >= 0) & (gcol_a < band_cols)
    sub_a = lax.broadcasted_iota(jnp.int32, (BLK, width), 0)

    start = PAD + ROWH + shift_r
    start_low = (start // BLK) * BLK
    row_roll = lax.rem(2 * BLK - (start - start_low), 2 * BLK)

    def emit(i, carry):
        r0 = pl.multiple_of(i * BLK, BLK)
        block = final[pl.ds(pl.multiple_of(start_low + r0, BLK), 2 * BLK), :]
        block = pltpu.roll(block, row_roll, 0)[:BLK]
        block = pltpu.roll(block, roll_by, 1)[:, :width]
        grow = prm[0] + shift_r + r0 + sub_a
        keep = col_in & (grow >= 0) & (grow < band_rows)
        align_out[pl.ds(r0, BLK), :] = jnp.where(keep, block, 0.0)
        return carry
    lax.fori_loop(0, rows // BLK, emit, 0)


def smooth(prm, tile, top, bot, side, band_rows, band_cols):
    rows, width = tile.shape
    ext_w = width + 2 * COLH
    buf = pltpu.VMEM((rows + 2 * ROWH + 2 * PAD, ext_w), jnp.float32)
    vspec = pl.BlockSpec(memory_space=pltpu.VMEM)
    return pl.pallas_call(
        functools.partial(smooth_kernel, band_rows, band_cols),
        out_shape=(jax.ShapeDtypeStruct((rows, width), jnp.float32),) * 2,
        in_specs=[pl.BlockSpec(memory_space=pltpu.SMEM)] + [vspec] * 4,
        out_specs=(vspec, vspec),
        scratch_shapes=[buf, buf, buf],
        compiler_params=pltpu.CompilerParams(vmem_limit_bytes=60 * 1024 * 1024),
        cost_estimate=pl.CostEstimate(flops=STEPS * 40 * (rows + 2 * ROWH) * ext_w, bytes_accessed=4 * 3 * rows * width, transcendentals=0),
    )(prm, tile, top, bot, side)


def from_behind(block, axis, distance):
    devices = range(lax.axis_size(axis))
    route = [((i - distance) % len(devices), i) for i in devices]
    return lax.ppermute(block, axis, route)


def from_grid(block, d_swath, d_col):
    swaths, cols = lax.axis_size("swath"), lax.axis_size("col")
    route = []
    for s in range(swaths):
        for c in range(cols):
            t, u = s + d_swath, c + d_col
            if 0 <= t < swaths and 0 <= u < cols:
                route.append((s * cols + c, t * cols + u))
    return lax.ppermute(block, ("swath", "col"), route)


def three_die(aligned, left_block, right_block):
    first_diff = aligned - left_block
    second_diff = aligned - right_block
    return jnp.maximum(jnp.minimum(first_diff, second_diff), 0.0) + jnp.minimum(
        jnp.maximum(first_diff, second_diff), 0.0
    )


def local(raw_band, section_offsets):
    col_count = lax.axis_size("col")
    swath_count = lax.axis_size("swath")
    row_total, die_width = raw_band.shape
    die_tile = lax.all_to_all(raw_band, "col", split_axis=1, concat_axis=1, tiled=True)
    swath_index = lax.axis_index("swath")
    col_index = lax.axis_index("col")
    band_rows = swath_count * row_total
    band_cols = col_count * die_width
    first_rows, last_rows = die_tile[:ROWH], die_tile[-ROWH:]
    first_cols, last_cols = die_tile[:, :COLH], die_tile[:, -COLH:]
    top = from_grid(last_rows, 1, 0)
    bot = from_grid(first_rows, -1, 0)
    right = jnp.concatenate(
        [from_grid(last_rows[:, :COLH], 1, -1), from_grid(first_cols, 0, -1), from_grid(first_rows[:, :COLH], -1, -1)], 0
    )
    left = jnp.concatenate(
        [from_grid(last_rows[:, -COLH:], 1, 1), from_grid(last_cols, 0, 1), from_grid(first_rows[:, -COLH:], -1, 1)], 0
    )
    side = jnp.concatenate([right, left], 1)
    die_ids = lax.broadcasted_iota(jnp.int32, section_offsets.shape, 0)
    own_shift = jnp.sum(jnp.where(die_ids == col_index, section_offsets, 0), axis=0)
    prm = jnp.stack(
        [swath_index * row_total, col_index * die_width, own_shift[0], own_shift[1]]
        + [jnp.int32(0)] * 4
    ).astype(jnp.int32)
    diffused, aligned = smooth(prm, die_tile, top, bot, side, band_rows, band_cols)
    left_block = from_behind(aligned, "col", 1)
    right_block = from_behind(aligned, "col", -1)
    defect = three_die(aligned, left_block, right_block)
    return (diffused, defect)


def solution(mesh):
    in_specs = (P("swath", "col"), P())
    out_specs = (P("swath", "col"), P("swath", "col"))
    return jax.shard_map(local, mesh=mesh, in_specs=in_specs, out_specs=out_specs, check_vma=False)
```

```python
import functools

import jax
import jax.numpy as jnp
from jax import lax
from jax.experimental import pallas as pl
from jax.experimental.pallas import tpu as pltpu
from jax.sharding import PartitionSpec as P

STEPS = 4
MAXOFF = 16
ROWH = 32
COLH = 64
PAD = 64
BLK = 64
step_rate = 0.2


def conduct_flux(differ):
    return differ / (1.0 + differ * differ)


def three_die(aligned, left_block, right_block):
    first_diff = aligned - left_block
    second_diff = aligned - right_block
    return jnp.maximum(jnp.minimum(first_diff, second_diff), 0.0) + jnp.minimum(
        jnp.maximum(first_diff, second_diff), 0.0
    )


def inspect_kernel(
    band_rows, band_cols, prm, tile, top, bot, side, diff_out, defect_out,
    s0, s1, s2, s3, fv_last, held, from_left, from_right, send_sem, recv_sem,
):
    rows, width = tile.shape
    ext_w = s0.shape[1]
    ext_r = rows + 2 * ROWH
    blocks = ext_r // BLK
    out_blocks = rows // BLK
    row_base = prm[0] - ROWH
    col_base = prm[1]
    shift_r = prm[2]
    shift_c = prm[3]
    mesh_ids = pl.DeviceIdType.MESH
    swath = lax.axis_index("swath")
    me = lax.axis_index("col")
    cols = lax.axis_size("col")
    right_dev = lax.rem(me + 1, cols)
    left_dev = lax.rem(me + cols - 1, cols)

    barrier = pltpu.get_barrier_semaphore()
    for partner in (left_dev, right_dev):
        pl.semaphore_signal(barrier, inc=1, device_id=(swath, partner), device_id_type=mesh_ids)
    pl.semaphore_wait(barrier, 2)

    zeros_pad = jnp.zeros((PAD, ext_w), jnp.float32)
    for buf in (s0, s1, s2, s3):
        buf[pl.ds(0, PAD), :] = zeros_pad
        buf[pl.ds(PAD + ext_r, PAD), :] = zeros_pad
    fv_last[...] = jnp.zeros(fv_last.shape, jnp.float32)
    s0[pl.ds(PAD, ROWH), pl.ds(0, width)] = top[...]
    s0[pl.ds(PAD + ROWH, rows), pl.ds(0, width)] = tile[...]
    s0[pl.ds(PAD + ROWH + rows, ROWH), pl.ds(0, width)] = bot[...]
    s0[pl.ds(PAD, ext_r), pl.ds(width, 2 * COLH)] = side[...]

    lane = lax.broadcasted_iota(jnp.int32, (BLK, ext_w), 1)
    gcol = col_base + lane - jnp.where(lane >= width + COLH, ext_w, 0)
    col_edge = (gcol >= 0) & (gcol <= band_cols - 2)
    sub = lax.broadcasted_iota(jnp.int32, (BLK, ext_w), 0)
    stages = (s0, s1, s2, s3, s0)

    def step_block(k, b):
        src, dst = stages[k], stages[k + 1]
        r0 = pl.multiple_of(PAD + b * BLK, BLK)
        pair = src[pl.ds(r0, 2 * BLK), :]
        here = pair[:BLK]
        below = pltpu.roll(pair, 2 * BLK - 1, 0)[:BLK]
        grow = row_base + b * BLK + sub
        row_edge = (grow >= 0) & (grow <= band_rows - 2)
        down = jnp.where(row_edge, conduct_flux(below - here), 0.0)
        above = pltpu.roll(fv_last[k], 1, 0)[0:1]
        up = jnp.where(sub == 0, above, pltpu.roll(down, 1, 0))
        fv_last[k] = down[BLK - 8:]
        right = pltpu.roll(here, ext_w - 1, 1)
        across = jnp.where(col_edge, conduct_flux(right - here), 0.0)
        left = pltpu.roll(across, 1, 1)
        dst[pl.ds(r0, BLK), :] = here + step_rate * ((down - up) + (across - left))

    roll_by = lax.rem(ext_w - shift_c, ext_w)
    gcol_a = col_base + shift_c + lax.broadcasted_iota(jnp.int32, (BLK, width), 1)
    col_in = (gcol_a >= 0) & (gcol_a < band_cols)
    sub_a = lax.broadcasted_iota(jnp.int32, (BLK, width), 0)
    row_roll = 2 * BLK - (ROWH + shift_r)

    def send(a, side_index):
        rows_a = pl.ds(pl.multiple_of(a * BLK, BLK), BLK)
        target = from_left if side_index == 0 else from_right
        return pltpu.make_async_remote_copy(
            src_ref=held.at[rows_a],
            dst_ref=target.at[rows_a],
            send_sem=send_sem.at[side_index, a],
            recv_sem=recv_sem.at[side_index, a],
            device_id=(swath, right_dev if side_index == 0 else left_dev),
            device_id_type=mesh_ids,
        )

    def emit(a):
        r0 = pl.multiple_of(PAD + a * BLK, BLK)
        block = s0[pl.ds(r0, 2 * BLK), :]
        block = pltpu.roll(block, row_roll, 0)[:BLK]
        block = pltpu.roll(block, roll_by, 1)[:, :width]
        grow = prm[0] + shift_r + a * BLK + sub_a
        keep = col_in & (grow >= 0) & (grow < band_rows)
        held[pl.ds(pl.multiple_of(a * BLK, BLK), BLK), :] = jnp.where(keep, block, 0.0)
        send(a, 0).start()
        send(a, 1).start()

    def wave(i, carry):
        for k in range(STEPS):
            b = i - k

            @pl.when((b >= 0) & (b < blocks))
            def _():
                step_block(k, b)

        a = i - STEPS

        @pl.when((a >= 0) & (a < out_blocks))
        def _():
            emit(a)

        return carry

    lax.fori_loop(0, blocks + STEPS, wave, 0)
    diff_out[...] = s0[pl.ds(PAD + ROWH, rows), pl.ds(0, width)]

    def finish(a, carry):
        for side_index in (0, 1):
            send(a, side_index).wait_recv()
        for side_index in (0, 1):
            send(a, side_index).wait_send()
        rows_a = pl.ds(pl.multiple_of(a * BLK, BLK), BLK)
        defect_out[rows_a, :] = three_die(held[rows_a, :], from_left[rows_a, :], from_right[rows_a, :])
        return carry

    lax.fori_loop(0, out_blocks, finish, 0)


def inspect(prm, tile, top, bot, side, band_rows, band_cols):
    rows, width = tile.shape
    ext_w = width + 2 * COLH
    out_blocks = rows // BLK
    buf = pltpu.VMEM((rows + 2 * ROWH + 2 * PAD, ext_w), jnp.float32)
    die = pltpu.VMEM((rows, width), jnp.float32)
    vspec = pl.BlockSpec(memory_space=pltpu.VMEM)
    return pl.pallas_call(
        functools.partial(inspect_kernel, band_rows, band_cols),
        out_shape=(jax.ShapeDtypeStruct((rows, width), jnp.float32),) * 2,
        in_specs=[pl.BlockSpec(memory_space=pltpu.SMEM)] + [vspec] * 4,
        out_specs=(vspec, vspec),
        scratch_shapes=[
            buf, buf, buf, buf,
            pltpu.VMEM((STEPS, 8, ext_w), jnp.float32),
            die, die, die,
            pltpu.SemaphoreType.DMA((2, out_blocks)),
            pltpu.SemaphoreType.DMA((2, out_blocks)),
        ],
        compiler_params=pltpu.CompilerParams(
            vmem_limit_bytes=64000 * 1024, collective_id=0, has_side_effects=True
        ),
        cost_estimate=pl.CostEstimate(
            flops=STEPS * 40 * (rows + 2 * ROWH) * ext_w, bytes_accessed=4 * 3 * rows * width, transcendentals=0
        ),
    )(prm, tile, top, bot, side)


def from_behind(block, axis, distance):
    devices = range(lax.axis_size(axis))
    route = [((i - distance) % len(devices), i) for i in devices]
    return lax.ppermute(block, axis, route)


def from_grid(block, d_swath, d_col):
    swaths, cols = lax.axis_size("swath"), lax.axis_size("col")
    route = []
    for s in range(swaths):
        for c in range(cols):
            t, u = s + d_swath, c + d_col
            if 0 <= t < swaths and 0 <= u < cols:
                route.append((s * cols + c, t * cols + u))
    return lax.ppermute(block, ("swath", "col"), route)


def local(raw_band, section_offsets):
    col_count = lax.axis_size("col")
    swath_count = lax.axis_size("swath")
    row_total, die_width = raw_band.shape
    die_tile = lax.all_to_all(raw_band, "col", split_axis=1, concat_axis=1, tiled=True)
    swath_index = lax.axis_index("swath")
    col_index = lax.axis_index("col")
    band_rows = swath_count * row_total
    band_cols = col_count * die_width
    first_rows, last_rows = die_tile[:ROWH], die_tile[-ROWH:]
    first_cols, last_cols = die_tile[:, :COLH], die_tile[:, -COLH:]
    top = from_grid(last_rows, 1, 0)
    bot = from_grid(first_rows, -1, 0)
    right = jnp.concatenate(
        [from_grid(last_rows[:, :COLH], 1, -1), from_grid(first_cols, 0, -1), from_grid(first_rows[:, :COLH], -1, -1)], 0
    )
    left = jnp.concatenate(
        [from_grid(last_rows[:, -COLH:], 1, 1), from_grid(last_cols, 0, 1), from_grid(first_rows[:, -COLH:], -1, 1)], 0
    )
    side = jnp.concatenate([right, left], 1)
    die_ids = lax.broadcasted_iota(jnp.int32, section_offsets.shape, 0)
    own_shift = jnp.sum(jnp.where(die_ids == col_index, section_offsets, 0), axis=0)
    prm = jnp.stack(
        [swath_index * row_total, col_index * die_width, own_shift[0], own_shift[1]]
        + [jnp.int32(0)] * 4
    ).astype(jnp.int32)
    return inspect(prm, die_tile, top, bot, side, band_rows, band_cols)


def solution(mesh):
    in_specs = (P("swath", "col"), P())
    out_specs = (P("swath", "col"), P("swath", "col"))
    return jax.shard_map(local, mesh=mesh, in_specs=in_specs, out_specs=out_specs, check_vma=False)
```

```python
import functools

import jax
import jax.numpy as jnp
from jax import lax
from jax.experimental import pallas as pl
from jax.experimental.pallas import tpu as pltpu
from jax.sharding import PartitionSpec as P

STEPS = 4
MAXOFF = 16
ROWH = 32
COLH = 128
PAD = 64
BLK = 64
step_rate = 0.2


def conduct_flux(differ):
    return differ / (1.0 + differ * differ)


def three_die(aligned, left_block, right_block):
    first_diff = aligned - left_block
    second_diff = aligned - right_block
    return jnp.maximum(jnp.minimum(first_diff, second_diff), 0.0) + jnp.minimum(
        jnp.maximum(first_diff, second_diff), 0.0
    )


def inspect_kernel(
    band_rows, band_cols, prm, tile, diff_out, defect_out,
    s0, s1, s2, s3, fv_last, held, from_left, from_right, send_sem, recv_sem, halo_send, halo_recv,
):
    rows, width = tile.shape
    ext_w = s0.shape[1]
    ext_r = rows + 2 * ROWH
    blocks = ext_r // BLK
    out_blocks = rows // BLK
    row_base = prm[0] - ROWH
    col_base = prm[1]
    shift_r = prm[2]
    shift_c = prm[3]
    mesh_ids = pl.DeviceIdType.MESH
    swath = lax.axis_index("swath")
    me = lax.axis_index("col")
    cols = lax.axis_size("col")
    swaths = lax.axis_size("swath")
    right_dev = lax.rem(me + 1, cols)
    left_dev = lax.rem(me + cols - 1, cols)
    below_dev = lax.rem(swath + 1, swaths)
    above_dev = lax.rem(swath + swaths - 1, swaths)

    top_rows, end_rows = pl.ds(0, ROWH), pl.ds(rows - ROWH, ROWH)
    first_cols, end_cols = pl.ds(0, COLH), pl.ds(width - COLH, COLH)
    all_rows, all_cols = pl.ds(0, rows), pl.ds(0, width)
    top_halo, bot_halo, mid_rows = pl.ds(PAD, ROWH), pl.ds(PAD + ROWH + rows, ROWH), pl.ds(PAD + ROWH, rows)
    right_halo, left_halo = pl.ds(width, COLH), pl.ds(width + COLH, COLH)
    halo_plan = (
        ((below_dev, me), (end_rows, all_cols), (top_halo, all_cols)),
        ((above_dev, me), (top_rows, all_cols), (bot_halo, all_cols)),
        ((swath, left_dev), (all_rows, first_cols), (mid_rows, right_halo)),
        ((swath, right_dev), (all_rows, end_cols), (mid_rows, left_halo)),
        ((below_dev, left_dev), (end_rows, first_cols), (top_halo, right_halo)),
        ((below_dev, right_dev), (end_rows, end_cols), (top_halo, left_halo)),
        ((above_dev, left_dev), (top_rows, first_cols), (bot_halo, right_halo)),
        ((above_dev, right_dev), (top_rows, end_cols), (bot_halo, left_halo)),
    )

    def halo_copy(n):
        target, src, dst = halo_plan[n]
        return pltpu.make_async_remote_copy(
            src_ref=tile.at[src],
            dst_ref=s0.at[dst],
            send_sem=halo_send.at[n],
            recv_sem=halo_recv.at[n],
            device_id=target,
            device_id_type=mesh_ids,
        )

    barrier = pltpu.get_barrier_semaphore()
    for target, _, _ in halo_plan:
        pl.semaphore_signal(barrier, inc=1, device_id=target, device_id_type=mesh_ids)
    pl.semaphore_wait(barrier, len(halo_plan))
    for n in range(len(halo_plan)):
        halo_copy(n).start()

    zeros_pad = jnp.zeros((PAD, ext_w), jnp.float32)
    for buf in (s0, s1, s2, s3):
        buf[pl.ds(0, PAD), :] = zeros_pad
        buf[pl.ds(PAD + ext_r, PAD), :] = zeros_pad
    fv_last[...] = jnp.zeros(fv_last.shape, jnp.float32)
    s0[mid_rows, all_cols] = tile[...]
    for n in range(len(halo_plan)):
        halo_copy(n).wait_recv()
    for n in range(len(halo_plan)):
        halo_copy(n).wait_send()

    lane = lax.broadcasted_iota(jnp.int32, (BLK, ext_w), 1)
    gcol = col_base + lane - jnp.where(lane >= width + COLH, ext_w, 0)
    col_edge = (gcol >= 0) & (gcol <= band_cols - 2)
    sub = lax.broadcasted_iota(jnp.int32, (BLK, ext_w), 0)
    stages = (s0, s1, s2, s3, s0)

    def step_block(k, b):
        src, dst = stages[k], stages[k + 1]
        r0 = pl.multiple_of(PAD + b * BLK, BLK)
        pair = src[pl.ds(r0, 2 * BLK), :]
        here = pair[:BLK]
        below = pltpu.roll(pair, 2 * BLK - 1, 0)[:BLK]
        grow = row_base + b * BLK + sub
        row_edge = (grow >= 0) & (grow <= band_rows - 2)
        down = jnp.where(row_edge, conduct_flux(below - here), 0.0)
        above = pltpu.roll(fv_last[k], 1, 0)[0:1]
        up = jnp.where(sub == 0, above, pltpu.roll(down, 1, 0))
        fv_last[k] = down[BLK - 8:]
        right = pltpu.roll(here, ext_w - 1, 1)
        across = jnp.where(col_edge, conduct_flux(right - here), 0.0)
        left = pltpu.roll(across, 1, 1)
        dst[pl.ds(r0, BLK), :] = here + step_rate * ((down - up) + (across - left))

    roll_by = lax.rem(ext_w - shift_c, ext_w)
    gcol_a = col_base + shift_c + lax.broadcasted_iota(jnp.int32, (BLK, width), 1)
    col_in = (gcol_a >= 0) & (gcol_a < band_cols)
    sub_a = lax.broadcasted_iota(jnp.int32, (BLK, width), 0)
    row_roll = 2 * BLK - (ROWH + shift_r)

    def send(a, side_index):
        rows_a = pl.ds(pl.multiple_of(a * BLK, BLK), BLK)
        target = from_left if side_index == 0 else from_right
        return pltpu.make_async_remote_copy(
            src_ref=held.at[rows_a],
            dst_ref=target.at[rows_a],
            send_sem=send_sem.at[side_index, a],
            recv_sem=recv_sem.at[side_index, a],
            device_id=(swath, right_dev if side_index == 0 else left_dev),
            device_id_type=mesh_ids,
        )

    def emit(a):
        r0 = pl.multiple_of(PAD + a * BLK, BLK)
        block = s0[pl.ds(r0, 2 * BLK), :]
        block = pltpu.roll(block, row_roll, 0)[:BLK]
        block = pltpu.roll(block, roll_by, 1)[:, :width]
        grow = prm[0] + shift_r + a * BLK + sub_a
        keep = col_in & (grow >= 0) & (grow < band_rows)
        held[pl.ds(pl.multiple_of(a * BLK, BLK), BLK), :] = jnp.where(keep, block, 0.0)
        send(a, 0).start()
        send(a, 1).start()

    def wave(i, carry):
        for k in range(STEPS):
            b = i - k

            @pl.when((b >= 0) & (b < blocks))
            def _():
                step_block(k, b)

        a = i - STEPS

        @pl.when((a >= 0) & (a < out_blocks))
        def _():
            emit(a)

        return carry

    lax.fori_loop(0, blocks + STEPS, wave, 0)
    diff_out[...] = s0[pl.ds(PAD + ROWH, rows), pl.ds(0, width)]

    def finish(a, carry):
        for side_index in (0, 1):
            send(a, side_index).wait_recv()
        for side_index in (0, 1):
            send(a, side_index).wait_send()
        rows_a = pl.ds(pl.multiple_of(a * BLK, BLK), BLK)
        defect_out[rows_a, :] = three_die(held[rows_a, :], from_left[rows_a, :], from_right[rows_a, :])
        return carry

    lax.fori_loop(0, out_blocks, finish, 0)


def inspect(prm, tile, band_rows, band_cols):
    rows, width = tile.shape
    ext_w = width + 2 * COLH
    out_blocks = rows // BLK
    buf = pltpu.VMEM((rows + 2 * ROWH + 2 * PAD, ext_w), jnp.float32)
    die = pltpu.VMEM((rows, width), jnp.float32)
    vspec = pl.BlockSpec(memory_space=pltpu.VMEM)
    return pl.pallas_call(
        functools.partial(inspect_kernel, band_rows, band_cols),
        out_shape=(jax.ShapeDtypeStruct((rows, width), jnp.float32),) * 2,
        in_specs=[pl.BlockSpec(memory_space=pltpu.SMEM), vspec],
        out_specs=(vspec, vspec),
        scratch_shapes=[
            buf, buf, buf, buf,
            pltpu.VMEM((STEPS, 8, ext_w), jnp.float32),
            die, die, die,
            pltpu.SemaphoreType.DMA((2, out_blocks)),
            pltpu.SemaphoreType.DMA((2, out_blocks)),
            pltpu.SemaphoreType.DMA((8,)),
            pltpu.SemaphoreType.DMA((8,)),
        ],
        compiler_params=pltpu.CompilerParams(
            vmem_limit_bytes=64000 * 1024, collective_id=0, has_side_effects=True
        ),
        cost_estimate=pl.CostEstimate(
            flops=STEPS * 40 * (rows + 2 * ROWH) * ext_w, bytes_accessed=4 * 3 * rows * width, transcendentals=0
        ),
    )(prm, tile)


def local(raw_band, section_offsets):
    col_count = lax.axis_size("col")
    swath_count = lax.axis_size("swath")
    row_total, die_width = raw_band.shape
    die_tile = lax.all_to_all(raw_band, "col", split_axis=1, concat_axis=1, tiled=True)
    swath_index = lax.axis_index("swath")
    col_index = lax.axis_index("col")
    band_rows = swath_count * row_total
    band_cols = col_count * die_width
    die_ids = lax.broadcasted_iota(jnp.int32, section_offsets.shape, 0)
    own_shift = jnp.sum(jnp.where(die_ids == col_index, section_offsets, 0), axis=0)
    prm = jnp.stack(
        [swath_index * row_total, col_index * die_width, own_shift[0], own_shift[1]]
        + [jnp.int32(0)] * 4
    ).astype(jnp.int32)
    return inspect(prm, die_tile, band_rows, band_cols)


def solution(mesh):
    in_specs = (P("swath", "col"), P())
    out_specs = (P("swath", "col"), P("swath", "col"))
    return jax.shard_map(local, mesh=mesh, in_specs=in_specs, out_specs=out_specs, check_vma=False)
```

```python
import functools

import jax
import jax.numpy as jnp
from jax import lax
from jax.experimental import pallas as pl
from jax.experimental.pallas import tpu as pltpu
from jax.sharding import PartitionSpec as P

STEPS = 4
MAXOFF = 16
ROWH = 32
COLH = 128
PAD = 64
BLK = 64
step_rate = 0.2


def conduct_flux(differ):
    return differ / (1.0 + differ * differ)


def three_die(aligned, left_block, right_block):
    first_diff = aligned - left_block
    second_diff = aligned - right_block
    return jnp.maximum(jnp.minimum(first_diff, second_diff), 0.0) + jnp.minimum(
        jnp.maximum(first_diff, second_diff), 0.0
    )


def inspect_kernel(
    band_rows, band_cols, prm, tile_top, tile_bot, diff_out, defect_out,
    s0, s1, s2, s3, fv_last, held, from_left, from_right, send_sem, recv_sem, halo_send, halo_recv,
):
    half, width = tile_top.shape
    rows = 2 * half
    ext_w = s0.shape[1]
    ext_r = rows + 2 * ROWH
    blocks = ext_r // BLK
    out_blocks = rows // BLK
    row_base = prm[0] - ROWH
    col_base = prm[1]
    shift_r = prm[2]
    shift_c = prm[3]
    mesh_ids = pl.DeviceIdType.MESH
    swath = lax.axis_index("swath")
    me = lax.axis_index("col")
    cols = lax.axis_size("col")
    swaths = lax.axis_size("swath")
    right_dev = lax.rem(me + 1, cols)
    left_dev = lax.rem(me + cols - 1, cols)
    below_dev = lax.rem(swath + 1, swaths)
    above_dev = lax.rem(swath + swaths - 1, swaths)

    top_rows, end_rows = pl.ds(0, ROWH), pl.ds(half - ROWH, ROWH)
    first_cols, end_cols = pl.ds(0, COLH), pl.ds(width - COLH, COLH)
    all_rows, all_cols = pl.ds(0, half), pl.ds(0, width)
    top_halo, bot_halo, mid_rows = pl.ds(PAD, ROWH), pl.ds(PAD + ROWH + rows, ROWH), pl.ds(PAD + ROWH, rows)
    right_halo, left_halo = pl.ds(width, COLH), pl.ds(width + COLH, COLH)
    halo_plan = (
        ((below_dev, me), (end_rows, all_cols), (top_halo, all_cols)),
        ((above_dev, me), (top_rows, all_cols), (bot_halo, all_cols)),
        ((swath, left_dev), (all_rows, first_cols), (pl.ds(PAD + ROWH, half), right_halo)),
        ((swath, right_dev), (all_rows, end_cols), (pl.ds(PAD + ROWH, half), left_halo)),
        ((swath, left_dev), (all_rows, first_cols), (pl.ds(PAD + ROWH + half, half), right_halo)),
        ((swath, right_dev), (all_rows, end_cols), (pl.ds(PAD + ROWH + half, half), left_halo)),
        ((below_dev, left_dev), (end_rows, first_cols), (top_halo, right_halo)),
        ((below_dev, right_dev), (end_rows, end_cols), (top_halo, left_halo)),
        ((above_dev, left_dev), (top_rows, first_cols), (bot_halo, right_halo)),
        ((above_dev, right_dev), (top_rows, end_cols), (bot_halo, left_halo)),
    )

    def halo_copy(n):
        target, src, dst = halo_plan[n]
        rows_src, cols_src = src
        tile = tile_bot if n in (0, 4, 5, 6, 7) else tile_top
        return pltpu.make_async_remote_copy(
            src_ref=tile.at[rows_src, cols_src],
            dst_ref=s0.at[dst],
            send_sem=halo_send.at[n],
            recv_sem=halo_recv.at[n],
            device_id=target,
            device_id_type=mesh_ids,
        )

    barrier = pltpu.get_barrier_semaphore()
    for target, _, _ in halo_plan:
        pl.semaphore_signal(barrier, inc=1, device_id=target, device_id_type=mesh_ids)
    pl.semaphore_wait(barrier, len(halo_plan))
    for n in range(len(halo_plan)):
        halo_copy(n).start()

    zeros_pad = jnp.zeros((PAD, ext_w), jnp.float32)
    for buf in (s0, s1, s2, s3):
        buf[pl.ds(0, PAD), :] = zeros_pad
        buf[pl.ds(PAD + ext_r, PAD), :] = zeros_pad
    fv_last[...] = jnp.zeros(fv_last.shape, jnp.float32)
    s0[pl.ds(PAD + ROWH, half), all_cols] = tile_top[...]
    s0[pl.ds(PAD + ROWH + half, half), all_cols] = tile_bot[...]
    for n in range(len(halo_plan)):
        halo_copy(n).wait_recv()
    for n in range(len(halo_plan)):
        halo_copy(n).wait_send()

    lane = lax.broadcasted_iota(jnp.int32, (BLK, ext_w), 1)
    gcol = col_base + lane - jnp.where(lane >= width + COLH, ext_w, 0)
    col_edge = (gcol >= 0) & (gcol <= band_cols - 2)
    sub = lax.broadcasted_iota(jnp.int32, (BLK, ext_w), 0)
    stages = (s0, s1, s2, s3, s0)

    def step_block(k, b):
        src, dst = stages[k], stages[k + 1]
        r0 = pl.multiple_of(PAD + b * BLK, BLK)
        pair = src[pl.ds(r0, 2 * BLK), :]
        here = pair[:BLK]
        below = pltpu.roll(pair, 2 * BLK - 1, 0)[:BLK]
        grow = row_base + b * BLK + sub
        row_edge = (grow >= 0) & (grow <= band_rows - 2)
        down = jnp.where(row_edge, conduct_flux(below - here), 0.0)
        above = pltpu.roll(fv_last[k], 1, 0)[0:1]
        up = jnp.where(sub == 0, above, pltpu.roll(down, 1, 0))
        fv_last[k] = down[BLK - 8:]
        right = pltpu.roll(here, ext_w - 1, 1)
        across = jnp.where(col_edge, conduct_flux(right - here), 0.0)
        left = pltpu.roll(across, 1, 1)
        dst[pl.ds(r0, BLK), :] = here + step_rate * ((down - up) + (across - left))

    roll_by = lax.rem(ext_w - shift_c, ext_w)
    gcol_a = col_base + shift_c + lax.broadcasted_iota(jnp.int32, (BLK, width), 1)
    col_in = (gcol_a >= 0) & (gcol_a < band_cols)
    sub_a = lax.broadcasted_iota(jnp.int32, (BLK, width), 0)
    row_roll = 2 * BLK - (ROWH + shift_r)

    def send(a, side_index):
        rows_a = pl.ds(pl.multiple_of(a * BLK, BLK), BLK)
        target = from_left if side_index == 0 else from_right
        return pltpu.make_async_remote_copy(
            src_ref=held.at[rows_a],
            dst_ref=target.at[rows_a],
            send_sem=send_sem.at[side_index, a],
            recv_sem=recv_sem.at[side_index, a],
            device_id=(swath, right_dev if side_index == 0 else left_dev),
            device_id_type=mesh_ids,
        )

    def emit(a):
        r0 = pl.multiple_of(PAD + a * BLK, BLK)
        block = s0[pl.ds(r0, 2 * BLK), :]
        block = pltpu.roll(block, row_roll, 0)[:BLK]
        block = pltpu.roll(block, roll_by, 1)[:, :width]
        grow = prm[0] + shift_r + a * BLK + sub_a
        keep = col_in & (grow >= 0) & (grow < band_rows)
        held[pl.ds(pl.multiple_of(a * BLK, BLK), BLK), :] = jnp.where(keep, block, 0.0)
        send(a, 0).start()
        send(a, 1).start()

    def wave(i, carry):
        for k in range(STEPS):
            b = i - k

            @pl.when((b >= 0) & (b < blocks))
            def _():
                step_block(k, b)

        a = i - STEPS

        @pl.when((a >= 0) & (a < out_blocks))
        def _():
            emit(a)

        return carry

    lax.fori_loop(0, blocks + STEPS, wave, 0)
    diff_out[...] = s0[pl.ds(PAD + ROWH, rows), pl.ds(0, width)]

    def finish(a, carry):
        for side_index in (0, 1):
            send(a, side_index).wait_recv()
        for side_index in (0, 1):
            send(a, side_index).wait_send()
        rows_a = pl.ds(pl.multiple_of(a * BLK, BLK), BLK)
        defect_out[rows_a, :] = three_die(held[rows_a, :], from_left[rows_a, :], from_right[rows_a, :])
        return carry

    lax.fori_loop(0, out_blocks, finish, 0)


def inspect(prm, tile_top, tile_bot, band_rows, band_cols):
    half, width = tile_top.shape
    rows = 2 * half
    ext_w = width + 2 * COLH
    out_blocks = rows // BLK
    buf = pltpu.VMEM((rows + 2 * ROWH + 2 * PAD, ext_w), jnp.float32)
    die = pltpu.VMEM((rows, width), jnp.float32)
    vspec = pl.BlockSpec(memory_space=pltpu.VMEM)
    return pl.pallas_call(
        functools.partial(inspect_kernel, band_rows, band_cols),
        out_shape=(jax.ShapeDtypeStruct((rows, width), jnp.float32),) * 2,
        in_specs=[pl.BlockSpec(memory_space=pltpu.SMEM), vspec, vspec],
        out_specs=(vspec, vspec),
        scratch_shapes=[
            buf, buf, buf, buf,
            pltpu.VMEM((STEPS, 8, ext_w), jnp.float32),
            die, die, die,
            pltpu.SemaphoreType.DMA((2, out_blocks)),
            pltpu.SemaphoreType.DMA((2, out_blocks)),
            pltpu.SemaphoreType.DMA((10,)),
            pltpu.SemaphoreType.DMA((10,)),
        ],
        compiler_params=pltpu.CompilerParams(
            vmem_limit_bytes=64000 * 1024, collective_id=0, has_side_effects=True
        ),
        cost_estimate=pl.CostEstimate(
            flops=STEPS * 40 * (rows + 2 * ROWH) * ext_w, bytes_accessed=4 * 3 * rows * width, transcendentals=0
        ),
    )(prm, tile_top, tile_bot)


def local(raw_band, section_offsets):
    col_count = lax.axis_size("col")
    swath_count = lax.axis_size("swath")
    row_total, die_width = raw_band.shape
    half = row_total // 2
    tile_top, tile_bot = (
        lax.all_to_all(part, "col", split_axis=1, concat_axis=1, tiled=True)
        for part in (raw_band[:half], raw_band[half:])
    )
    swath_index = lax.axis_index("swath")
    col_index = lax.axis_index("col")
    band_rows = swath_count * row_total
    band_cols = col_count * die_width
    die_ids = lax.broadcasted_iota(jnp.int32, section_offsets.shape, 0)
    own_shift = jnp.sum(jnp.where(die_ids == col_index, section_offsets, 0), axis=0)
    prm = jnp.stack(
        [swath_index * row_total, col_index * die_width, own_shift[0], own_shift[1]]
        + [jnp.int32(0)] * 4
    ).astype(jnp.int32)
    return inspect(prm, tile_top, tile_bot, band_rows, band_cols)


def solution(mesh):
    in_specs = (P("swath", "col"), P())
    out_specs = (P("swath", "col"), P("swath", "col"))
    return jax.shard_map(local, mesh=mesh, in_specs=in_specs, out_specs=out_specs, check_vma=False)
```

```python
import functools

import jax
import jax.numpy as jnp
from jax import lax
from jax.experimental import pallas as pl
from jax.experimental.pallas import tpu as pltpu
from jax.sharding import PartitionSpec as P

STEPS = 4
MAXOFF = 16
ROWH = 32
COLH = 128
PAD = 64
BLK = 64
step_rate = 0.2


def conduct_flux(differ):
    return differ / (1.0 + differ * differ)


def three_die(aligned, left_block, right_block):
    first_diff = aligned - left_block
    second_diff = aligned - right_block
    return jnp.maximum(jnp.minimum(first_diff, second_diff), 0.0) + jnp.minimum(
        jnp.maximum(first_diff, second_diff), 0.0
    )


def inspect_kernel(
    band_rows, band_cols, prm, tile, diff_out, defect_out,
    s0, s1, s2, s3, fv_last, held, from_left, from_right, send_sem, recv_sem, halo_send, halo_recv, load_sem,
    defect_buf, out_sem,
):
    rows, width = tile.shape
    ext_w = s0.shape[1]
    ext_r = rows + 2 * ROWH
    blocks = ext_r // BLK
    out_blocks = rows // BLK
    row_base = prm[0] - ROWH
    col_base = prm[1]
    shift_r = prm[2]
    shift_c = prm[3]
    mesh_ids = pl.DeviceIdType.MESH
    swath = lax.axis_index("swath")
    me = lax.axis_index("col")
    cols = lax.axis_size("col")
    swaths = lax.axis_size("swath")
    right_dev = lax.rem(me + 1, cols)
    left_dev = lax.rem(me + cols - 1, cols)
    below_dev = lax.rem(swath + 1, swaths)
    above_dev = lax.rem(swath + swaths - 1, swaths)

    top_rows, end_rows = pl.ds(0, ROWH), pl.ds(rows - ROWH, ROWH)
    first_cols, end_cols = pl.ds(0, COLH), pl.ds(width - COLH, COLH)
    all_rows, all_cols = pl.ds(0, rows), pl.ds(0, width)
    top_halo, bot_halo, mid_rows = pl.ds(PAD, ROWH), pl.ds(PAD + ROWH + rows, ROWH), pl.ds(PAD + ROWH, rows)
    right_halo, left_halo = pl.ds(width, COLH), pl.ds(width + COLH, COLH)
    halo_plan = (
        ((below_dev, me), (end_rows, all_cols), (top_halo, all_cols)),
        ((above_dev, me), (top_rows, all_cols), (bot_halo, all_cols)),
        ((swath, left_dev), (all_rows, first_cols), (mid_rows, right_halo)),
        ((swath, right_dev), (all_rows, end_cols), (mid_rows, left_halo)),
        ((below_dev, left_dev), (end_rows, first_cols), (top_halo, right_halo)),
        ((below_dev, right_dev), (end_rows, end_cols), (top_halo, left_halo)),
        ((above_dev, left_dev), (top_rows, first_cols), (bot_halo, right_halo)),
        ((above_dev, right_dev), (top_rows, end_cols), (bot_halo, left_halo)),
    )

    def halo_copy(n):
        target, src, dst = halo_plan[n]
        return pltpu.make_async_remote_copy(
            src_ref=tile.at[src],
            dst_ref=s0.at[dst],
            send_sem=halo_send.at[n],
            recv_sem=halo_recv.at[n],
            device_id=target,
            device_id_type=mesh_ids,
        )

    load = pltpu.make_async_copy(tile, s0.at[mid_rows, all_cols], load_sem.at[0])
    load.start()
    barrier = pltpu.get_barrier_semaphore()
    for target, _, _ in halo_plan:
        pl.semaphore_signal(barrier, inc=1, device_id=target, device_id_type=mesh_ids)
    pl.semaphore_wait(barrier, len(halo_plan))
    for n in range(len(halo_plan)):
        halo_copy(n).start()

    zeros_pad = jnp.zeros((PAD, ext_w), jnp.float32)
    for buf in (s0, s1, s2, s3):
        buf[pl.ds(0, PAD), :] = zeros_pad
        buf[pl.ds(PAD + ext_r, PAD), :] = zeros_pad
    fv_last[...] = jnp.zeros(fv_last.shape, jnp.float32)
    load.wait()
    for n in range(len(halo_plan)):
        halo_copy(n).wait_recv()
    for n in range(len(halo_plan)):
        halo_copy(n).wait_send()

    lane = lax.broadcasted_iota(jnp.int32, (BLK, ext_w), 1)
    gcol = col_base + lane - jnp.where(lane >= width + COLH, ext_w, 0)
    col_edge = (gcol >= 0) & (gcol <= band_cols - 2)
    sub = lax.broadcasted_iota(jnp.int32, (BLK, ext_w), 0)
    stages = (s0, s1, s2, s3, s0)

    def step_block(k, b):
        src, dst = stages[k], stages[k + 1]
        r0 = pl.multiple_of(PAD + b * BLK, BLK)
        pair = src[pl.ds(r0, 2 * BLK), :]
        here = pair[:BLK]
        below = pltpu.roll(pair, 2 * BLK - 1, 0)[:BLK]
        grow = row_base + b * BLK + sub
        row_edge = (grow >= 0) & (grow <= band_rows - 2)
        down = jnp.where(row_edge, conduct_flux(below - here), 0.0)
        above = pltpu.roll(fv_last[k], 1, 0)[0:1]
        up = jnp.where(sub == 0, above, pltpu.roll(down, 1, 0))
        fv_last[k] = down[BLK - 8:]
        right = pltpu.roll(here, ext_w - 1, 1)
        across = jnp.where(col_edge, conduct_flux(right - here), 0.0)
        left = pltpu.roll(across, 1, 1)
        dst[pl.ds(r0, BLK), :] = here + step_rate * ((down - up) + (across - left))

    roll_by = lax.rem(ext_w - shift_c, ext_w)
    gcol_a = col_base + shift_c + lax.broadcasted_iota(jnp.int32, (BLK, width), 1)
    col_in = (gcol_a >= 0) & (gcol_a < band_cols)
    sub_a = lax.broadcasted_iota(jnp.int32, (BLK, width), 0)
    row_roll = 2 * BLK - (ROWH + shift_r)

    def send(a, side_index):
        rows_a = pl.ds(pl.multiple_of(a * BLK, BLK), BLK)
        target = from_left if side_index == 0 else from_right
        return pltpu.make_async_remote_copy(
            src_ref=held.at[rows_a],
            dst_ref=target.at[rows_a],
            send_sem=send_sem.at[side_index, a],
            recv_sem=recv_sem.at[side_index, a],
            device_id=(swath, right_dev if side_index == 0 else left_dev),
            device_id_type=mesh_ids,
        )

    def emit(a):
        r0 = pl.multiple_of(PAD + a * BLK, BLK)
        block = s0[pl.ds(r0, 2 * BLK), :]
        block = pltpu.roll(block, row_roll, 0)[:BLK]
        block = pltpu.roll(block, roll_by, 1)[:, :width]
        grow = prm[0] + shift_r + a * BLK + sub_a
        keep = col_in & (grow >= 0) & (grow < band_rows)
        held[pl.ds(pl.multiple_of(a * BLK, BLK), BLK), :] = jnp.where(keep, block, 0.0)
        send(a, 0).start()
        send(a, 1).start()

    def wave(i, carry):
        for k in range(STEPS):
            b = i - k

            @pl.when((b >= 0) & (b < blocks))
            def _():
                step_block(k, b)

        a = i - STEPS

        @pl.when((a >= 0) & (a < out_blocks))
        def _():
            emit(a)

        return carry

    lax.fori_loop(0, blocks + STEPS, wave, 0)
    diff_copy = pltpu.make_async_copy(s0.at[mid_rows, all_cols], diff_out, out_sem.at[0])
    diff_copy.start()

    def finish(a, carry):
        for side_index in (0, 1):
            send(a, side_index).wait_recv()
        for side_index in (0, 1):
            send(a, side_index).wait_send()
        rows_a = pl.ds(pl.multiple_of(a * BLK, BLK), BLK)
        defect_buf[rows_a, :] = three_die(held[rows_a, :], from_left[rows_a, :], from_right[rows_a, :])
        return carry

    lax.fori_loop(0, out_blocks, finish, 0)
    defect_copy = pltpu.make_async_copy(defect_buf, defect_out, out_sem.at[1])
    defect_copy.start()
    diff_copy.wait()
    defect_copy.wait()


def inspect(prm, tile, band_rows, band_cols):
    rows, width = tile.shape
    ext_w = width + 2 * COLH
    out_blocks = rows // BLK
    buf = pltpu.VMEM((rows + 2 * ROWH + 2 * PAD, ext_w), jnp.float32)
    die = pltpu.VMEM((rows, width), jnp.float32)
    return pl.pallas_call(
        functools.partial(inspect_kernel, band_rows, band_cols),
        out_shape=(jax.ShapeDtypeStruct((rows, width), jnp.float32),) * 2,
        in_specs=[pl.BlockSpec(memory_space=pltpu.SMEM), pl.BlockSpec(memory_space=pl.ANY)],
        out_specs=(pl.BlockSpec(memory_space=pl.ANY), pl.BlockSpec(memory_space=pl.ANY)),
        scratch_shapes=[
            buf, buf, buf, buf,
            pltpu.VMEM((STEPS, 8, ext_w), jnp.float32),
            die, die, die,
            pltpu.SemaphoreType.DMA((2, out_blocks)),
            pltpu.SemaphoreType.DMA((2, out_blocks)),
            pltpu.SemaphoreType.DMA((8,)),
            pltpu.SemaphoreType.DMA((8,)),
            pltpu.SemaphoreType.DMA((1,)),
            die,
            pltpu.SemaphoreType.DMA((2,)),
        ],
        compiler_params=pltpu.CompilerParams(
            vmem_limit_bytes=64000 * 1024, collective_id=0, has_side_effects=True
        ),
        cost_estimate=pl.CostEstimate(
            flops=STEPS * 40 * (rows + 2 * ROWH) * ext_w, bytes_accessed=4 * 3 * rows * width, transcendentals=0
        ),
    )(prm, tile)


def local(raw_band, section_offsets):
    col_count = lax.axis_size("col")
    swath_count = lax.axis_size("swath")
    row_total, die_width = raw_band.shape
    die_tile = lax.all_to_all(raw_band, "col", split_axis=1, concat_axis=1, tiled=True)
    swath_index = lax.axis_index("swath")
    col_index = lax.axis_index("col")
    band_rows = swath_count * row_total
    band_cols = col_count * die_width
    die_ids = lax.broadcasted_iota(jnp.int32, section_offsets.shape, 0)
    own_shift = jnp.sum(jnp.where(die_ids == col_index, section_offsets, 0), axis=0)
    prm = jnp.stack(
        [swath_index * row_total, col_index * die_width, own_shift[0], own_shift[1]]
        + [jnp.int32(0)] * 4
    ).astype(jnp.int32)
    return inspect(prm, die_tile, band_rows, band_cols)


def solution(mesh):
    in_specs = (P("swath", "col"), P())
    out_specs = (P("swath", "col"), P("swath", "col"))
    return jax.shard_map(local, mesh=mesh, in_specs=in_specs, out_specs=out_specs, check_vma=False)
```

```python
import functools

import jax
import jax.numpy as jnp
from jax import lax
from jax.experimental import pallas as pl
from jax.experimental.pallas import tpu as pltpu
from jax.sharding import PartitionSpec as P

STEPS = 4
MAXOFF = 16
ROWH = 32
COLH = 128
PAD = 64
BLK = 64
step_rate = 0.2


def conduct_flux(differ):
    return differ / (1.0 + differ * differ)


def three_die(aligned, left_block, right_block):
    first_diff = aligned - left_block
    second_diff = aligned - right_block
    return jnp.maximum(jnp.minimum(first_diff, second_diff), 0.0) + jnp.minimum(
        jnp.maximum(first_diff, second_diff), 0.0
    )


def inspect_kernel(
    band_rows, band_cols, prm, raw_t, diff_out, defect_out,
    s0, s1, s2, s3, fv_last, held, from_left, from_right, send_sem, recv_sem, halo_send, halo_recv, load_sem,
    defect_buf, out_sem, tile_t,
):
    width, rows = raw_t.shape
    ext_w = s0.shape[1]
    ext_r = rows + 2 * ROWH
    blocks = ext_r // BLK
    out_blocks = rows // BLK
    row_base = prm[0] - ROWH
    col_base = prm[1]
    shift_r = prm[2]
    shift_c = prm[3]
    mesh_ids = pl.DeviceIdType.MESH
    swath = lax.axis_index("swath")
    me = lax.axis_index("col")
    cols = lax.axis_size("col")
    swaths = lax.axis_size("swath")
    right_dev = lax.rem(me + 1, cols)
    left_dev = lax.rem(me + cols - 1, cols)
    below_dev = lax.rem(swath + 1, swaths)
    above_dev = lax.rem(swath + swaths - 1, swaths)

    top_rows, end_rows = pl.ds(0, ROWH), pl.ds(rows - ROWH, ROWH)
    first_cols, end_cols = pl.ds(0, COLH), pl.ds(width - COLH, COLH)
    all_rows, all_cols = pl.ds(0, rows), pl.ds(0, width)
    top_halo, bot_halo, mid_rows = pl.ds(PAD, ROWH), pl.ds(PAD + ROWH + rows, ROWH), pl.ds(PAD + ROWH, rows)
    right_halo, left_halo = pl.ds(width, COLH), pl.ds(width + COLH, COLH)
    halo_plan = (
        ((below_dev, me), (end_rows, all_cols), (top_halo, all_cols)),
        ((above_dev, me), (top_rows, all_cols), (bot_halo, all_cols)),
        ((swath, left_dev), (all_rows, first_cols), (mid_rows, right_halo)),
        ((swath, right_dev), (all_rows, end_cols), (mid_rows, left_halo)),
        ((below_dev, left_dev), (end_rows, first_cols), (top_halo, right_halo)),
        ((below_dev, right_dev), (end_rows, end_cols), (top_halo, left_halo)),
        ((above_dev, left_dev), (top_rows, first_cols), (bot_halo, right_halo)),
        ((above_dev, right_dev), (top_rows, end_cols), (bot_halo, left_halo)),
    )

    def halo_copy(n):
        target, src, dst = halo_plan[n]
        rows_src, cols_src = src
        return pltpu.make_async_remote_copy(
            src_ref=s0.at[pl.ds(PAD + ROWH + rows_src.start, rows_src.size), cols_src],
            dst_ref=s0.at[dst],
            send_sem=halo_send.at[n],
            recv_sem=halo_recv.at[n],
            device_id=target,
            device_id_type=mesh_ids,
        )

    load = pltpu.make_async_copy(raw_t, tile_t, load_sem.at[0])
    load.start()
    barrier = pltpu.get_barrier_semaphore()
    for target, _, _ in halo_plan:
        pl.semaphore_signal(barrier, inc=1, device_id=target, device_id_type=mesh_ids)
    pl.semaphore_wait(barrier, len(halo_plan))
    load.wait()

    def flip_rows(i, carry):
        for j in range(width // 128):
            block = tile_t[pl.ds(j * 128, 128), pl.ds(pl.multiple_of(i * 128, 128), 128)]
            s0[pl.ds(pl.multiple_of(PAD + ROWH + i * 128, 8), 128), pl.ds(j * 128, 128)] = block.T
        return carry

    lax.fori_loop(0, rows // 128, flip_rows, 0)
    for n in range(len(halo_plan)):
        halo_copy(n).start()

    zeros_pad = jnp.zeros((PAD, ext_w), jnp.float32)
    for buf in (s0, s1, s2, s3):
        buf[pl.ds(0, PAD), :] = zeros_pad
        buf[pl.ds(PAD + ext_r, PAD), :] = zeros_pad
    fv_last[...] = jnp.zeros(fv_last.shape, jnp.float32)
    for n in range(len(halo_plan)):
        halo_copy(n).wait_recv()
    for n in range(len(halo_plan)):
        halo_copy(n).wait_send()

    lane = lax.broadcasted_iota(jnp.int32, (BLK, ext_w), 1)
    gcol = col_base + lane - jnp.where(lane >= width + COLH, ext_w, 0)
    col_edge = (gcol >= 0) & (gcol <= band_cols - 2)
    sub = lax.broadcasted_iota(jnp.int32, (BLK, ext_w), 0)
    stages = (s0, s1, s2, s3, s0)

    def step_block(k, b):
        src, dst = stages[k], stages[k + 1]
        r0 = pl.multiple_of(PAD + b * BLK, BLK)
        pair = src[pl.ds(r0, 2 * BLK), :]
        here = pair[:BLK]
        below = pltpu.roll(pair, 2 * BLK - 1, 0)[:BLK]
        grow = row_base + b * BLK + sub
        row_edge = (grow >= 0) & (grow <= band_rows - 2)
        down = jnp.where(row_edge, conduct_flux(below - here), 0.0)
        above = pltpu.roll(fv_last[k], 1, 0)[0:1]
        up = jnp.where(sub == 0, above, pltpu.roll(down, 1, 0))
        fv_last[k] = down[BLK - 8:]
        right = pltpu.roll(here, ext_w - 1, 1)
        across = jnp.where(col_edge, conduct_flux(right - here), 0.0)
        left = pltpu.roll(across, 1, 1)
        dst[pl.ds(r0, BLK), :] = here + step_rate * ((down - up) + (across - left))

    roll_by = lax.rem(ext_w - shift_c, ext_w)
    gcol_a = col_base + shift_c + lax.broadcasted_iota(jnp.int32, (BLK, width), 1)
    col_in = (gcol_a >= 0) & (gcol_a < band_cols)
    sub_a = lax.broadcasted_iota(jnp.int32, (BLK, width), 0)
    row_roll = 2 * BLK - (ROWH + shift_r)

    def send(a, side_index):
        rows_a = pl.ds(pl.multiple_of(a * BLK, BLK), BLK)
        target = from_left if side_index == 0 else from_right
        return pltpu.make_async_remote_copy(
            src_ref=held.at[rows_a],
            dst_ref=target.at[rows_a],
            send_sem=send_sem.at[side_index, a],
            recv_sem=recv_sem.at[side_index, a],
            device_id=(swath, right_dev if side_index == 0 else left_dev),
            device_id_type=mesh_ids,
        )

    def emit(a):
        r0 = pl.multiple_of(PAD + a * BLK, BLK)
        block = s0[pl.ds(r0, 2 * BLK), :]
        block = pltpu.roll(block, row_roll, 0)[:BLK]
        block = pltpu.roll(block, roll_by, 1)[:, :width]
        grow = prm[0] + shift_r + a * BLK + sub_a
        keep = col_in & (grow >= 0) & (grow < band_rows)
        held[pl.ds(pl.multiple_of(a * BLK, BLK), BLK), :] = jnp.where(keep, block, 0.0)
        send(a, 0).start()
        send(a, 1).start()

    def wave(i, carry):
        for k in range(STEPS):
            b = i - k

            @pl.when((b >= 0) & (b < blocks))
            def _():
                step_block(k, b)

        a = i - STEPS

        @pl.when((a >= 0) & (a < out_blocks))
        def _():
            emit(a)

        return carry

    lax.fori_loop(0, blocks + STEPS, wave, 0)
    diff_copy = pltpu.make_async_copy(s0.at[mid_rows, all_cols], diff_out, out_sem.at[0])
    diff_copy.start()

    def finish(a, carry):
        for side_index in (0, 1):
            send(a, side_index).wait_recv()
        for side_index in (0, 1):
            send(a, side_index).wait_send()
        rows_a = pl.ds(pl.multiple_of(a * BLK, BLK), BLK)
        defect_buf[rows_a, :] = three_die(held[rows_a, :], from_left[rows_a, :], from_right[rows_a, :])
        return carry

    lax.fori_loop(0, out_blocks, finish, 0)
    defect_copy = pltpu.make_async_copy(defect_buf, defect_out, out_sem.at[1])
    defect_copy.start()
    diff_copy.wait()
    defect_copy.wait()


def inspect(prm, raw_t, band_rows, band_cols):
    width, rows = raw_t.shape
    ext_w = width + 2 * COLH
    out_blocks = rows // BLK
    buf = pltpu.VMEM((rows + 2 * ROWH + 2 * PAD, ext_w), jnp.float32)
    die = pltpu.VMEM((rows, width), jnp.float32)
    return pl.pallas_call(
        functools.partial(inspect_kernel, band_rows, band_cols),
        out_shape=(jax.ShapeDtypeStruct((rows, width), jnp.float32),) * 2,
        in_specs=[pl.BlockSpec(memory_space=pltpu.SMEM), pl.BlockSpec(memory_space=pl.ANY)],
        out_specs=(pl.BlockSpec(memory_space=pl.ANY), pl.BlockSpec(memory_space=pl.ANY)),
        scratch_shapes=[
            buf, buf, buf, buf,
            pltpu.VMEM((STEPS, 8, ext_w), jnp.float32),
            die, die, die,
            pltpu.SemaphoreType.DMA((2, out_blocks)),
            pltpu.SemaphoreType.DMA((2, out_blocks)),
            pltpu.SemaphoreType.DMA((8,)),
            pltpu.SemaphoreType.DMA((8,)),
            pltpu.SemaphoreType.DMA((1,)),
            die,
            pltpu.SemaphoreType.DMA((2,)),
            die,
        ],
        compiler_params=pltpu.CompilerParams(
            vmem_limit_bytes=64000 * 1024, collective_id=0, has_side_effects=True
        ),
        cost_estimate=pl.CostEstimate(
            flops=STEPS * 40 * (rows + 2 * ROWH) * ext_w, bytes_accessed=4 * 3 * rows * width, transcendentals=0
        ),
    )(prm, raw_t)


def local(raw_band, section_offsets):
    col_count = lax.axis_size("col")
    swath_count = lax.axis_size("swath")
    row_total, die_width = raw_band.shape
    raw_t = lax.all_to_all(raw_band.T, "col", split_axis=0, concat_axis=0, tiled=True)
    swath_index = lax.axis_index("swath")
    col_index = lax.axis_index("col")
    band_rows = swath_count * row_total
    band_cols = col_count * die_width
    die_ids = lax.broadcasted_iota(jnp.int32, section_offsets.shape, 0)
    own_shift = jnp.sum(jnp.where(die_ids == col_index, section_offsets, 0), axis=0)
    prm = jnp.stack(
        [swath_index * row_total, col_index * die_width, own_shift[0], own_shift[1]]
        + [jnp.int32(0)] * 4
    ).astype(jnp.int32)
    return inspect(prm, raw_t, band_rows, band_cols)


def solution(mesh):
    in_specs = (P("swath", "col"), P())
    out_specs = (P("swath", "col"), P("swath", "col"))
    return jax.shard_map(local, mesh=mesh, in_specs=in_specs, out_specs=out_specs, check_vma=False)
```

```python
import functools

import jax
import jax.numpy as jnp
from jax import lax
from jax.experimental import pallas as pl
from jax.experimental.pallas import tpu as pltpu
from jax.sharding import PartitionSpec as P

STEPS = 4
MAXOFF = 16
ROWH = 32
COLH = 128
PAD = 64
BLK = 64
step_rate = 0.2


def conduct_flux(differ):
    return differ / (1.0 + differ * differ)


def three_die(aligned, left_block, right_block):
    first_diff = aligned - left_block
    second_diff = aligned - right_block
    return jnp.maximum(jnp.minimum(first_diff, second_diff), 0.0) + jnp.minimum(
        jnp.maximum(first_diff, second_diff), 0.0
    )


def inspect_kernel(
    band_rows, band_cols, prm, raw_t, diff_out, defect_out,
    s0, s1, s2, s3, fv_last, held, from_left, from_right, send_sem, recv_sem, halo_send, halo_recv, load_sem,
    defect_buf, out_sem, tile_t,
):
    width, rows = raw_t.shape
    ext_w = s0.shape[1]
    ext_r = rows + 2 * ROWH
    blocks = ext_r // BLK
    out_blocks = rows // BLK
    row_base = prm[0] - ROWH
    col_base = prm[1]
    shift_r = prm[2]
    shift_c = prm[3]
    mesh_ids = pl.DeviceIdType.MESH
    swath = lax.axis_index("swath")
    me = lax.axis_index("col")
    cols = lax.axis_size("col")
    swaths = lax.axis_size("swath")
    right_dev = lax.rem(me + 1, cols)
    left_dev = lax.rem(me + cols - 1, cols)
    below_dev = lax.rem(swath + 1, swaths)
    above_dev = lax.rem(swath + swaths - 1, swaths)

    top_rows, end_rows = pl.ds(0, ROWH), pl.ds(rows - ROWH, ROWH)
    first_cols, end_cols = pl.ds(0, COLH), pl.ds(width - COLH, COLH)
    all_rows, all_cols = pl.ds(0, rows), pl.ds(0, width)
    top_halo, bot_halo, mid_rows = pl.ds(PAD, ROWH), pl.ds(PAD + ROWH + rows, ROWH), pl.ds(PAD + ROWH, rows)
    right_halo, left_halo = pl.ds(width, COLH), pl.ds(width + COLH, COLH)
    halo_plan = (
        ((below_dev, me), (end_rows, all_cols), (top_halo, all_cols)),
        ((above_dev, me), (top_rows, all_cols), (bot_halo, all_cols)),
        ((swath, left_dev), (all_rows, first_cols), (mid_rows, right_halo)),
        ((swath, right_dev), (all_rows, end_cols), (mid_rows, left_halo)),
        ((below_dev, left_dev), (end_rows, first_cols), (top_halo, right_halo)),
        ((below_dev, right_dev), (end_rows, end_cols), (top_halo, left_halo)),
        ((above_dev, left_dev), (top_rows, first_cols), (bot_halo, right_halo)),
        ((above_dev, right_dev), (top_rows, end_cols), (bot_halo, left_halo)),
    )

    def halo_copy(n):
        target, src, dst = halo_plan[n]
        rows_src, cols_src = src
        return pltpu.make_async_remote_copy(
            src_ref=s0.at[pl.ds(PAD + ROWH + rows_src.start, rows_src.size), cols_src],
            dst_ref=s0.at[dst],
            send_sem=halo_send.at[n],
            recv_sem=halo_recv.at[n],
            device_id=target,
            device_id_type=mesh_ids,
        )

    strips = [
        pltpu.make_async_copy(raw_t.at[pl.ds(j * 128, 128)], tile_t.at[pl.ds(j * 128, 128)], load_sem.at[j])
        for j in range(width // 128)
    ]
    for strip in strips:
        strip.start()
    barrier = pltpu.get_barrier_semaphore()
    for target, _, _ in halo_plan:
        pl.semaphore_signal(barrier, inc=1, device_id=target, device_id_type=mesh_ids)
    pl.semaphore_wait(barrier, len(halo_plan))

    for j, strip in enumerate(strips):
        strip.wait()

        def flip_strip(i, carry, j=j):
            block = tile_t[pl.ds(j * 128, 128), pl.ds(pl.multiple_of(i * 128, 128), 128)]
            s0[pl.ds(pl.multiple_of(PAD + ROWH + i * 128, 8), 128), pl.ds(j * 128, 128)] = block.T
            return carry

        lax.fori_loop(0, rows // 128, flip_strip, 0)
    for n in range(len(halo_plan)):
        halo_copy(n).start()

    zeros_pad = jnp.zeros((PAD, ext_w), jnp.float32)
    for buf in (s0, s1, s2, s3):
        buf[pl.ds(0, PAD), :] = zeros_pad
        buf[pl.ds(PAD + ext_r, PAD), :] = zeros_pad
    fv_last[...] = jnp.zeros(fv_last.shape, jnp.float32)
    for n in range(len(halo_plan)):
        halo_copy(n).wait_recv()
    for n in range(len(halo_plan)):
        halo_copy(n).wait_send()

    lane = lax.broadcasted_iota(jnp.int32, (BLK, ext_w), 1)
    gcol = col_base + lane - jnp.where(lane >= width + COLH, ext_w, 0)
    col_edge = (gcol >= 0) & (gcol <= band_cols - 2)
    sub = lax.broadcasted_iota(jnp.int32, (BLK, ext_w), 0)
    stages = (s0, s1, s2, s3, s0)

    def step_block(k, b):
        src, dst = stages[k], stages[k + 1]
        r0 = pl.multiple_of(PAD + b * BLK, BLK)
        pair = src[pl.ds(r0, 2 * BLK), :]
        here = pair[:BLK]
        below = pltpu.roll(pair, 2 * BLK - 1, 0)[:BLK]
        grow = row_base + b * BLK + sub
        row_edge = (grow >= 0) & (grow <= band_rows - 2)
        down = jnp.where(row_edge, conduct_flux(below - here), 0.0)
        above = pltpu.roll(fv_last[k], 1, 0)[0:1]
        up = jnp.where(sub == 0, above, pltpu.roll(down, 1, 0))
        fv_last[k] = down[BLK - 8:]
        right = pltpu.roll(here, ext_w - 1, 1)
        across = jnp.where(col_edge, conduct_flux(right - here), 0.0)
        left = pltpu.roll(across, 1, 1)
        dst[pl.ds(r0, BLK), :] = here + step_rate * ((down - up) + (across - left))

    roll_by = lax.rem(ext_w - shift_c, ext_w)
    gcol_a = col_base + shift_c + lax.broadcasted_iota(jnp.int32, (BLK, width), 1)
    col_in = (gcol_a >= 0) & (gcol_a < band_cols)
    sub_a = lax.broadcasted_iota(jnp.int32, (BLK, width), 0)
    row_roll = 2 * BLK - (ROWH + shift_r)

    def send(a, side_index):
        rows_a = pl.ds(pl.multiple_of(a * BLK, BLK), BLK)
        target = from_left if side_index == 0 else from_right
        return pltpu.make_async_remote_copy(
            src_ref=held.at[rows_a],
            dst_ref=target.at[rows_a],
            send_sem=send_sem.at[side_index, a],
            recv_sem=recv_sem.at[side_index, a],
            device_id=(swath, right_dev if side_index == 0 else left_dev),
            device_id_type=mesh_ids,
        )

    def emit(a):
        r0 = pl.multiple_of(PAD + a * BLK, BLK)
        block = s0[pl.ds(r0, 2 * BLK), :]
        block = pltpu.roll(block, row_roll, 0)[:BLK]
        block = pltpu.roll(block, roll_by, 1)[:, :width]
        grow = prm[0] + shift_r + a * BLK + sub_a
        keep = col_in & (grow >= 0) & (grow < band_rows)
        held[pl.ds(pl.multiple_of(a * BLK, BLK), BLK), :] = jnp.where(keep, block, 0.0)
        send(a, 0).start()
        send(a, 1).start()

    def wave(i, carry):
        for k in range(STEPS):
            b = i - k

            @pl.when((b >= 0) & (b < blocks))
            def _():
                step_block(k, b)

        a = i - STEPS

        @pl.when((a >= 0) & (a < out_blocks))
        def _():
            emit(a)

        return carry

    lax.fori_loop(0, blocks + STEPS, wave, 0)
    diff_copy = pltpu.make_async_copy(s0.at[mid_rows, all_cols], diff_out, out_sem.at[0])
    diff_copy.start()

    def finish(a, carry):
        for side_index in (0, 1):
            send(a, side_index).wait_recv()
        for side_index in (0, 1):
            send(a, side_index).wait_send()
        rows_a = pl.ds(pl.multiple_of(a * BLK, BLK), BLK)
        defect_buf[rows_a, :] = three_die(held[rows_a, :], from_left[rows_a, :], from_right[rows_a, :])
        pltpu.make_async_copy(defect_buf.at[rows_a], defect_out.at[rows_a], out_sem.at[1]).start()
        return carry

    lax.fori_loop(0, out_blocks, finish, 0)
    defect_copy = pltpu.make_async_copy(defect_buf, defect_out, out_sem.at[1])
    diff_copy.wait()
    defect_copy.wait()


def inspect(prm, raw_t, band_rows, band_cols):
    width, rows = raw_t.shape
    ext_w = width + 2 * COLH
    out_blocks = rows // BLK
    buf = pltpu.VMEM((rows + 2 * ROWH + 2 * PAD, ext_w), jnp.float32)
    die = pltpu.VMEM((rows, width), jnp.float32)
    return pl.pallas_call(
        functools.partial(inspect_kernel, band_rows, band_cols),
        out_shape=(jax.ShapeDtypeStruct((rows, width), jnp.float32),) * 2,
        in_specs=[pl.BlockSpec(memory_space=pltpu.SMEM), pl.BlockSpec(memory_space=pl.ANY)],
        out_specs=(pl.BlockSpec(memory_space=pl.ANY), pl.BlockSpec(memory_space=pl.ANY)),
        scratch_shapes=[
            buf, buf, buf, buf,
            pltpu.VMEM((STEPS, 8, ext_w), jnp.float32),
            die, die, die,
            pltpu.SemaphoreType.DMA((2, out_blocks)),
            pltpu.SemaphoreType.DMA((2, out_blocks)),
            pltpu.SemaphoreType.DMA((8,)),
            pltpu.SemaphoreType.DMA((8,)),
            pltpu.SemaphoreType.DMA((width // 128,)),
            die,
            pltpu.SemaphoreType.DMA((2,)),
            die,
        ],
        compiler_params=pltpu.CompilerParams(
            vmem_limit_bytes=64000 * 1024, collective_id=0, has_side_effects=True
        ),
        cost_estimate=pl.CostEstimate(
            flops=STEPS * 40 * (rows + 2 * ROWH) * ext_w, bytes_accessed=4 * 3 * rows * width, transcendentals=0
        ),
    )(prm, raw_t)


def local(raw_band, section_offsets):
    col_count = lax.axis_size("col")
    swath_count = lax.axis_size("swath")
    row_total, die_width = raw_band.shape
    raw_t = lax.all_to_all(raw_band.T, "col", split_axis=0, concat_axis=0, tiled=True)
    swath_index = lax.axis_index("swath")
    col_index = lax.axis_index("col")
    band_rows = swath_count * row_total
    band_cols = col_count * die_width
    die_ids = lax.broadcasted_iota(jnp.int32, section_offsets.shape, 0)
    own_shift = jnp.sum(jnp.where(die_ids == col_index, section_offsets, 0), axis=0)
    prm = jnp.stack(
        [swath_index * row_total, col_index * die_width, own_shift[0], own_shift[1]]
        + [jnp.int32(0)] * 4
    ).astype(jnp.int32)
    return inspect(prm, raw_t, band_rows, band_cols)


def solution(mesh):
    in_specs = (P("swath", "col"), P())
    out_specs = (P("swath", "col"), P("swath", "col"))
    return jax.shard_map(local, mesh=mesh, in_specs=in_specs, out_specs=out_specs, check_vma=False)
```

```python
import functools

import jax
import jax.numpy as jnp
from jax import lax
from jax.experimental import pallas as pl
from jax.experimental.pallas import tpu as pltpu
from jax.sharding import PartitionSpec as P

STEPS = 4
MAXOFF = 16
ROWH = 32
COLH = 128
PAD = 64
BLK = 64
step_rate = 0.2


def conduct_flux(differ):
    return differ / (1.0 + differ * differ)


def three_die(aligned, left_block, right_block):
    first_diff = aligned - left_block
    second_diff = aligned - right_block
    return jnp.maximum(jnp.minimum(first_diff, second_diff), 0.0) + jnp.minimum(
        jnp.maximum(first_diff, second_diff), 0.0
    )


def inspect_kernel(
    band_rows, band_cols, prm, raw_t, diff_out, defect_out,
    s0, s1, s2, s3, fv_last, held, from_left, from_right, send_sem, recv_sem, halo_send, halo_recv, load_sem,
    defect_buf, out_sem, tile_t,
):
    width, rows = raw_t.shape
    ext_w = s0.shape[1]
    ext_r = rows + 2 * ROWH
    blocks = ext_r // BLK
    out_blocks = rows // BLK
    row_base = prm[0] - ROWH
    col_base = prm[1]
    shift_r = prm[2]
    shift_c = prm[3]
    mesh_ids = pl.DeviceIdType.MESH
    swath = lax.axis_index("swath")
    me = lax.axis_index("col")
    cols = lax.axis_size("col")
    swaths = lax.axis_size("swath")
    right_dev = lax.rem(me + 1, cols)
    left_dev = lax.rem(me + cols - 1, cols)
    below_dev = lax.rem(swath + 1, swaths)
    above_dev = lax.rem(swath + swaths - 1, swaths)

    top_rows, end_rows = pl.ds(0, ROWH), pl.ds(rows - ROWH, ROWH)
    first_cols, end_cols = pl.ds(0, COLH), pl.ds(width - COLH, COLH)
    all_rows, all_cols = pl.ds(0, rows), pl.ds(0, width)
    top_halo, bot_halo, mid_rows = pl.ds(PAD, ROWH), pl.ds(PAD + ROWH + rows, ROWH), pl.ds(PAD + ROWH, rows)
    right_halo, left_halo = pl.ds(width, COLH), pl.ds(width + COLH, COLH)
    halo_plan = (
        ((below_dev, me), (end_rows, all_cols), (top_halo, all_cols)),
        ((above_dev, me), (top_rows, all_cols), (bot_halo, all_cols)),
        ((swath, left_dev), (all_rows, first_cols), (mid_rows, right_halo)),
        ((swath, right_dev), (all_rows, end_cols), (mid_rows, left_halo)),
        ((below_dev, left_dev), (end_rows, first_cols), (top_halo, right_halo)),
        ((below_dev, right_dev), (end_rows, end_cols), (top_halo, left_halo)),
        ((above_dev, left_dev), (top_rows, first_cols), (bot_halo, right_halo)),
        ((above_dev, right_dev), (top_rows, end_cols), (bot_halo, left_halo)),
    )

    def halo_copy(n):
        target, src, dst = halo_plan[n]
        rows_src, cols_src = src
        return pltpu.make_async_remote_copy(
            src_ref=s0.at[pl.ds(PAD + ROWH + rows_src.start, rows_src.size), cols_src],
            dst_ref=s0.at[dst],
            send_sem=halo_send.at[n],
            recv_sem=halo_recv.at[n],
            device_id=target,
            device_id_type=mesh_ids,
        )

    load = pltpu.make_async_copy(raw_t, tile_t, load_sem.at[0])
    load.start()
    barrier = pltpu.get_barrier_semaphore()
    for target, _, _ in halo_plan:
        pl.semaphore_signal(barrier, inc=1, device_id=target, device_id_type=mesh_ids)
    pl.semaphore_wait(barrier, len(halo_plan))
    load.wait()

    def flip_rows(i, carry):
        for j in range(width // 128):
            block = tile_t[pl.ds(j * 128, 128), pl.ds(pl.multiple_of(i * 128, 128), 128)]
            s0[pl.ds(pl.multiple_of(PAD + ROWH + i * 128, 8), 128), pl.ds(j * 128, 128)] = block.T
        return carry

    lax.fori_loop(0, rows // 128, flip_rows, 0)
    for n in range(len(halo_plan)):
        halo_copy(n).start()

    zeros_pad = jnp.zeros((PAD, ext_w), jnp.float32)
    for buf in (s0, s1, s2, s3):
        buf[pl.ds(0, PAD), :] = zeros_pad
        buf[pl.ds(PAD + ext_r, PAD), :] = zeros_pad
    fv_last[...] = jnp.zeros(fv_last.shape, jnp.float32)
    for n in range(len(halo_plan)):
        halo_copy(n).wait_recv()
    for n in range(len(halo_plan)):
        halo_copy(n).wait_send()

    lane = lax.broadcasted_iota(jnp.int32, (BLK, ext_w), 1)
    gcol = col_base + lane - jnp.where(lane >= width + COLH, ext_w, 0)
    col_edge = (gcol >= 0) & (gcol <= band_cols - 2)
    sub = lax.broadcasted_iota(jnp.int32, (BLK, ext_w), 0)
    stages = (s0, s1, s2, s3, s0)

    def step_block(k, b):
        src, dst = stages[k], stages[k + 1]
        r0 = pl.multiple_of(PAD + b * BLK, BLK)
        pair = src[pl.ds(r0, 2 * BLK), :]
        here = pair[:BLK]
        below = pltpu.roll(pair, 2 * BLK - 1, 0)[:BLK]
        grow = row_base + b * BLK + sub
        row_edge = (grow >= 0) & (grow <= band_rows - 2)
        down = jnp.where(row_edge, conduct_flux(below - here), 0.0)
        above = pltpu.roll(fv_last[k], 1, 0)[0:1]
        up = jnp.where(sub == 0, above, pltpu.roll(down, 1, 0))
        fv_last[k] = down[BLK - 8:]
        right = pltpu.roll(here, ext_w - 1, 1)
        across = jnp.where(col_edge, conduct_flux(right - here), 0.0)
        left = pltpu.roll(across, 1, 1)
        dst[pl.ds(r0, BLK), :] = here + step_rate * ((down - up) + (across - left))

    roll_by = lax.rem(ext_w - shift_c, ext_w)
    gcol_a = col_base + shift_c + lax.broadcasted_iota(jnp.int32, (BLK, width), 1)
    col_in = (gcol_a >= 0) & (gcol_a < band_cols)
    sub_a = lax.broadcasted_iota(jnp.int32, (BLK, width), 0)
    row_roll = 2 * BLK - (ROWH + shift_r)

    def send(a, side_index):
        rows_a = pl.ds(pl.multiple_of(a * BLK, BLK), BLK)
        target = from_left if side_index == 0 else from_right
        return pltpu.make_async_remote_copy(
            src_ref=held.at[rows_a],
            dst_ref=target.at[rows_a],
            send_sem=send_sem.at[side_index, a],
            recv_sem=recv_sem.at[side_index, a],
            device_id=(swath, right_dev if side_index == 0 else left_dev),
            device_id_type=mesh_ids,
        )

    def emit(a):
        r0 = pl.multiple_of(PAD + a * BLK, BLK)
        block = s0[pl.ds(r0, 2 * BLK), :]
        block = pltpu.roll(block, row_roll, 0)[:BLK]
        block = pltpu.roll(block, roll_by, 1)[:, :width]
        grow = prm[0] + shift_r + a * BLK + sub_a
        keep = col_in & (grow >= 0) & (grow < band_rows)
        held[pl.ds(pl.multiple_of(a * BLK, BLK), BLK), :] = jnp.where(keep, block, 0.0)
        send(a, 0).start()
        send(a, 1).start()

    def wave(i, carry):
        for k in range(STEPS):
            b = i - k

            @pl.when((b >= 0) & (b < blocks))
            def _():
                step_block(k, b)

        a = i - STEPS

        @pl.when((a >= 0) & (a < out_blocks))
        def _():
            emit(a)

        return carry

    lax.fori_loop(0, blocks + STEPS, wave, 0)
    diff_copy = pltpu.make_async_copy(s0.at[mid_rows, all_cols], diff_out, out_sem.at[0])
    diff_copy.start()

    def finish(a, carry):
        for side_index in (0, 1):
            send(a, side_index).wait_recv()
        for side_index in (0, 1):
            send(a, side_index).wait_send()
        rows_a = pl.ds(pl.multiple_of(a * BLK, BLK), BLK)
        defect_buf[rows_a, :] = three_die(held[rows_a, :], from_left[rows_a, :], from_right[rows_a, :])
        pltpu.make_async_copy(defect_buf.at[rows_a], defect_out.at[rows_a], out_sem.at[1]).start()
        return carry

    lax.fori_loop(0, out_blocks, finish, 0)
    defect_copy = pltpu.make_async_copy(defect_buf, defect_out, out_sem.at[1])
    diff_copy.wait()
    defect_copy.wait()


def inspect(prm, raw_t, band_rows, band_cols):
    width, rows = raw_t.shape
    ext_w = width + 2 * COLH
    out_blocks = rows // BLK
    buf = pltpu.VMEM((rows + 2 * ROWH + 2 * PAD, ext_w), jnp.float32)
    die = pltpu.VMEM((rows, width), jnp.float32)
    return pl.pallas_call(
        functools.partial(inspect_kernel, band_rows, band_cols),
        out_shape=(jax.ShapeDtypeStruct((rows, width), jnp.float32),) * 2,
        in_specs=[pl.BlockSpec(memory_space=pltpu.SMEM), pl.BlockSpec(memory_space=pl.ANY)],
        out_specs=(pl.BlockSpec(memory_space=pl.ANY), pl.BlockSpec(memory_space=pl.ANY)),
        scratch_shapes=[
            buf, buf, buf, buf,
            pltpu.VMEM((STEPS, 8, ext_w), jnp.float32),
            die, die, die,
            pltpu.SemaphoreType.DMA((2, out_blocks)),
            pltpu.SemaphoreType.DMA((2, out_blocks)),
            pltpu.SemaphoreType.DMA((8,)),
            pltpu.SemaphoreType.DMA((8,)),
            pltpu.SemaphoreType.DMA((1,)),
            die,
            pltpu.SemaphoreType.DMA((2,)),
            die,
        ],
        compiler_params=pltpu.CompilerParams(
            vmem_limit_bytes=64000 * 1024, collective_id=0, has_side_effects=True
        ),
        cost_estimate=pl.CostEstimate(
            flops=STEPS * 40 * (rows + 2 * ROWH) * ext_w, bytes_accessed=4 * 3 * rows * width, transcendentals=0
        ),
    )(prm, raw_t)


def local(raw_band, section_offsets):
    col_count = lax.axis_size("col")
    swath_count = lax.axis_size("swath")
    row_total, die_width = raw_band.shape
    raw_t = lax.all_to_all(raw_band.T, "col", split_axis=0, concat_axis=0, tiled=True)
    swath_index = lax.axis_index("swath")
    col_index = lax.axis_index("col")
    band_rows = swath_count * row_total
    band_cols = col_count * die_width
    die_ids = lax.broadcasted_iota(jnp.int32, section_offsets.shape, 0)
    own_shift = jnp.sum(jnp.where(die_ids == col_index, section_offsets, 0), axis=0)
    prm = jnp.stack(
        [swath_index * row_total, col_index * die_width, own_shift[0], own_shift[1]]
        + [jnp.int32(0)] * 4
    ).astype(jnp.int32)
    return inspect(prm, raw_t, band_rows, band_cols)


def solution(mesh):
    in_specs = (P("swath", "col"), P())
    out_specs = (P("swath", "col"), P("swath", "col"))
    return jax.shard_map(local, mesh=mesh, in_specs=in_specs, out_specs=out_specs, check_vma=False)
```

```python
import functools

import jax
import jax.numpy as jnp
from jax import lax
from jax.experimental import pallas as pl
from jax.experimental.pallas import tpu as pltpu
from jax.sharding import PartitionSpec as P

STEPS = 4
MAXOFF = 16
ROWH = 32
COLH = 128
PAD = 64
BLK = 64
step_rate = 0.2


def conduct_flux(differ):
    return differ / (1.0 + differ * differ)


def three_die(aligned, left_block, right_block):
    first_diff = aligned - left_block
    second_diff = aligned - right_block
    return jnp.maximum(jnp.minimum(first_diff, second_diff), 0.0) + jnp.minimum(
        jnp.maximum(first_diff, second_diff), 0.0
    )


def inspect_kernel(
    band_rows, band_cols, prm, raw_t, diff_out, defect_out,
    s0, s1, s2, s3, fv_last, held, from_left, from_right, send_sem, recv_sem, halo_send, halo_recv, load_sem,
    defect_buf, out_sem, tile_t,
):
    width, rows = raw_t.shape
    ext_w = s0.shape[1]
    ext_r = rows + 2 * ROWH
    blocks = ext_r // BLK
    out_blocks = rows // BLK
    row_base = prm[0] - ROWH
    col_base = prm[1]
    shift_r = prm[2]
    shift_c = prm[3]
    mesh_ids = pl.DeviceIdType.MESH
    swath = lax.axis_index("swath")
    me = lax.axis_index("col")
    cols = lax.axis_size("col")
    swaths = lax.axis_size("swath")
    right_dev = lax.rem(me + 1, cols)
    left_dev = lax.rem(me + cols - 1, cols)
    below_dev = lax.rem(swath + 1, swaths)
    above_dev = lax.rem(swath + swaths - 1, swaths)

    top_rows, end_rows = pl.ds(0, ROWH), pl.ds(rows - ROWH, ROWH)
    first_cols, end_cols = pl.ds(0, COLH), pl.ds(width - COLH, COLH)
    all_rows, all_cols = pl.ds(0, rows), pl.ds(0, width)
    top_halo, bot_halo, mid_rows = pl.ds(PAD, ROWH), pl.ds(PAD + ROWH + rows, ROWH), pl.ds(PAD + ROWH, rows)
    right_halo, left_halo = pl.ds(width, COLH), pl.ds(width + COLH, COLH)
    halo_plan = (
        ((below_dev, me), (end_rows, all_cols), (top_halo, all_cols)),
        ((above_dev, me), (top_rows, all_cols), (bot_halo, all_cols)),
        ((swath, left_dev), (all_rows, first_cols), (mid_rows, right_halo)),
        ((swath, right_dev), (all_rows, end_cols), (mid_rows, left_halo)),
        ((below_dev, left_dev), (end_rows, first_cols), (top_halo, right_halo)),
        ((below_dev, right_dev), (end_rows, end_cols), (top_halo, left_halo)),
        ((above_dev, left_dev), (top_rows, first_cols), (bot_halo, right_halo)),
        ((above_dev, right_dev), (top_rows, end_cols), (bot_halo, left_halo)),
    )

    def halo_copy(n):
        target, src, dst = halo_plan[n]
        rows_src, cols_src = src
        return pltpu.make_async_remote_copy(
            src_ref=s0.at[pl.ds(PAD + ROWH + rows_src.start, rows_src.size), cols_src],
            dst_ref=s0.at[dst],
            send_sem=halo_send.at[n],
            recv_sem=halo_recv.at[n],
            device_id=target,
            device_id_type=mesh_ids,
        )

    load = pltpu.make_async_copy(raw_t, tile_t, load_sem.at[0])
    load.start()
    barrier = pltpu.get_barrier_semaphore()
    for target, _, _ in halo_plan:
        pl.semaphore_signal(barrier, inc=1, device_id=target, device_id_type=mesh_ids)
    pl.semaphore_wait(barrier, len(halo_plan))
    load.wait()

    def flip(i, j):
        block = tile_t[pl.ds(j * 128, 128), pl.ds(pl.multiple_of(i * 128, 128), 128)]
        s0[pl.ds(pl.multiple_of(PAD + ROWH + i * 128, 8), 128), pl.ds(j * 128, 128)] = block.T

    row_bands, col_bands = rows // 128, width // 128
    for i in range(row_bands):
        for j in range(col_bands):
            if i in (0, row_bands - 1) or j in (0, col_bands - 1):
                flip(i, j)
    for n in range(len(halo_plan)):
        halo_copy(n).start()

    def flip_inner(i, carry):
        for j in range(1, col_bands - 1):
            flip(i, j)
        return carry

    lax.fori_loop(1, row_bands - 1, flip_inner, 0)

    zeros_pad = jnp.zeros((PAD, ext_w), jnp.float32)
    for buf in (s0, s1, s2, s3):
        buf[pl.ds(0, PAD), :] = zeros_pad
        buf[pl.ds(PAD + ext_r, PAD), :] = zeros_pad
    fv_last[...] = jnp.zeros(fv_last.shape, jnp.float32)
    for n in range(len(halo_plan)):
        halo_copy(n).wait_recv()
    for n in range(len(halo_plan)):
        halo_copy(n).wait_send()

    lane = lax.broadcasted_iota(jnp.int32, (BLK, ext_w), 1)
    gcol = col_base + lane - jnp.where(lane >= width + COLH, ext_w, 0)
    col_edge = (gcol >= 0) & (gcol <= band_cols - 2)
    sub = lax.broadcasted_iota(jnp.int32, (BLK, ext_w), 0)
    stages = (s0, s1, s2, s3, s0)

    def step_block(k, b):
        src, dst = stages[k], stages[k + 1]
        r0 = pl.multiple_of(PAD + b * BLK, BLK)
        pair = src[pl.ds(r0, 2 * BLK), :]
        here = pair[:BLK]
        below = pltpu.roll(pair, 2 * BLK - 1, 0)[:BLK]
        grow = row_base + b * BLK + sub
        row_edge = (grow >= 0) & (grow <= band_rows - 2)
        down = jnp.where(row_edge, conduct_flux(below - here), 0.0)
        above = pltpu.roll(fv_last[k], 1, 0)[0:1]
        up = jnp.where(sub == 0, above, pltpu.roll(down, 1, 0))
        fv_last[k] = down[BLK - 8:]
        right = pltpu.roll(here, ext_w - 1, 1)
        across = jnp.where(col_edge, conduct_flux(right - here), 0.0)
        left = pltpu.roll(across, 1, 1)
        dst[pl.ds(r0, BLK), :] = here + step_rate * ((down - up) + (across - left))

    roll_by = lax.rem(ext_w - shift_c, ext_w)
    gcol_a = col_base + shift_c + lax.broadcasted_iota(jnp.int32, (BLK, width), 1)
    col_in = (gcol_a >= 0) & (gcol_a < band_cols)
    sub_a = lax.broadcasted_iota(jnp.int32, (BLK, width), 0)
    row_roll = 2 * BLK - (ROWH + shift_r)

    def send(a, side_index):
        rows_a = pl.ds(pl.multiple_of(a * BLK, BLK), BLK)
        target = from_left if side_index == 0 else from_right
        return pltpu.make_async_remote_copy(
            src_ref=held.at[rows_a],
            dst_ref=target.at[rows_a],
            send_sem=send_sem.at[side_index, a],
            recv_sem=recv_sem.at[side_index, a],
            device_id=(swath, right_dev if side_index == 0 else left_dev),
            device_id_type=mesh_ids,
        )

    def emit(a):
        r0 = pl.multiple_of(PAD + a * BLK, BLK)
        block = s0[pl.ds(r0, 2 * BLK), :]
        block = pltpu.roll(block, row_roll, 0)[:BLK]
        block = pltpu.roll(block, roll_by, 1)[:, :width]
        grow = prm[0] + shift_r + a * BLK + sub_a
        keep = col_in & (grow >= 0) & (grow < band_rows)
        held[pl.ds(pl.multiple_of(a * BLK, BLK), BLK), :] = jnp.where(keep, block, 0.0)
        send(a, 0).start()
        send(a, 1).start()

    def wave(i, carry):
        for k in range(STEPS):
            b = i - k

            @pl.when((b >= 0) & (b < blocks))
            def _():
                step_block(k, b)

        a = i - STEPS

        @pl.when((a >= 0) & (a < out_blocks))
        def _():
            emit(a)

        return carry

    lax.fori_loop(0, blocks + STEPS, wave, 0)
    diff_copy = pltpu.make_async_copy(s0.at[mid_rows, all_cols], diff_out, out_sem.at[0])
    diff_copy.start()

    def finish(a, carry):
        for side_index in (0, 1):
            send(a, side_index).wait_recv()
        for side_index in (0, 1):
            send(a, side_index).wait_send()
        rows_a = pl.ds(pl.multiple_of(a * BLK, BLK), BLK)
        defect_buf[rows_a, :] = three_die(held[rows_a, :], from_left[rows_a, :], from_right[rows_a, :])
        pltpu.make_async_copy(defect_buf.at[rows_a], defect_out.at[rows_a], out_sem.at[1]).start()
        return carry

    lax.fori_loop(0, out_blocks, finish, 0)
    defect_copy = pltpu.make_async_copy(defect_buf, defect_out, out_sem.at[1])
    diff_copy.wait()
    defect_copy.wait()


def inspect(prm, raw_t, band_rows, band_cols):
    width, rows = raw_t.shape
    ext_w = width + 2 * COLH
    out_blocks = rows // BLK
    buf = pltpu.VMEM((rows + 2 * ROWH + 2 * PAD, ext_w), jnp.float32)
    die = pltpu.VMEM((rows, width), jnp.float32)
    return pl.pallas_call(
        functools.partial(inspect_kernel, band_rows, band_cols),
        out_shape=(jax.ShapeDtypeStruct((rows, width), jnp.float32),) * 2,
        in_specs=[pl.BlockSpec(memory_space=pltpu.SMEM), pl.BlockSpec(memory_space=pl.ANY)],
        out_specs=(pl.BlockSpec(memory_space=pl.ANY), pl.BlockSpec(memory_space=pl.ANY)),
        scratch_shapes=[
            buf, buf, buf, buf,
            pltpu.VMEM((STEPS, 8, ext_w), jnp.float32),
            die, die, die,
            pltpu.SemaphoreType.DMA((2, out_blocks)),
            pltpu.SemaphoreType.DMA((2, out_blocks)),
            pltpu.SemaphoreType.DMA((8,)),
            pltpu.SemaphoreType.DMA((8,)),
            pltpu.SemaphoreType.DMA((1,)),
            die,
            pltpu.SemaphoreType.DMA((2,)),
            die,
        ],
        compiler_params=pltpu.CompilerParams(
            vmem_limit_bytes=64000 * 1024, collective_id=0, has_side_effects=True
        ),
        cost_estimate=pl.CostEstimate(
            flops=STEPS * 40 * (rows + 2 * ROWH) * ext_w, bytes_accessed=4 * 3 * rows * width, transcendentals=0
        ),
    )(prm, raw_t)


def local(raw_band, section_offsets):
    col_count = lax.axis_size("col")
    swath_count = lax.axis_size("swath")
    row_total, die_width = raw_band.shape
    raw_t = lax.all_to_all(raw_band.T, "col", split_axis=0, concat_axis=0, tiled=True)
    swath_index = lax.axis_index("swath")
    col_index = lax.axis_index("col")
    band_rows = swath_count * row_total
    band_cols = col_count * die_width
    die_ids = lax.broadcasted_iota(jnp.int32, section_offsets.shape, 0)
    own_shift = jnp.sum(jnp.where(die_ids == col_index, section_offsets, 0), axis=0)
    prm = jnp.stack(
        [swath_index * row_total, col_index * die_width, own_shift[0], own_shift[1]]
        + [jnp.int32(0)] * 4
    ).astype(jnp.int32)
    return inspect(prm, raw_t, band_rows, band_cols)


def solution(mesh):
    in_specs = (P("swath", "col"), P())
    out_specs = (P("swath", "col"), P("swath", "col"))
    return jax.shard_map(local, mesh=mesh, in_specs=in_specs, out_specs=out_specs, check_vma=False)
```

```python
import functools

import jax
import jax.numpy as jnp
from jax import lax
from jax.experimental import pallas as pl
from jax.experimental.pallas import tpu as pltpu
from jax.sharding import PartitionSpec as P

STEPS = 4
MAXOFF = 16
ROWH = 32
COLH = 128
PAD = 64
BLK = 64
step_rate = 0.2


def conduct_flux(differ):
    return differ / (1.0 + differ * differ)


def three_die(aligned, left_block, right_block):
    first_diff = aligned - left_block
    second_diff = aligned - right_block
    return jnp.maximum(jnp.minimum(first_diff, second_diff), 0.0) + jnp.minimum(
        jnp.maximum(first_diff, second_diff), 0.0
    )


def inspect_kernel(
    band_rows, band_cols, prm, raw_t, diff_out, defect_out,
    s0, s1, s2, s3, fv_last, held, from_left, from_right, send_sem, recv_sem, halo_send, halo_recv, load_sem,
    defect_buf, out_sem, tile_t,
):
    width, rows = raw_t.shape
    ext_w = s0.shape[1]
    ext_r = rows + 2 * ROWH
    blocks = ext_r // BLK
    out_blocks = rows // BLK
    row_base = prm[0] - ROWH
    col_base = prm[1]
    shift_r = prm[2]
    shift_c = prm[3]
    mesh_ids = pl.DeviceIdType.MESH
    swath = lax.axis_index("swath")
    me = lax.axis_index("col")
    cols = lax.axis_size("col")
    swaths = lax.axis_size("swath")
    right_dev = lax.rem(me + 1, cols)
    left_dev = lax.rem(me + cols - 1, cols)
    below_dev = lax.rem(swath + 1, swaths)
    above_dev = lax.rem(swath + swaths - 1, swaths)

    top_rows, end_rows = pl.ds(0, ROWH), pl.ds(rows - ROWH, ROWH)
    first_cols, end_cols = pl.ds(0, COLH), pl.ds(width - COLH, COLH)
    all_rows, all_cols = pl.ds(0, rows), pl.ds(0, width)
    top_halo, bot_halo, mid_rows = pl.ds(PAD, ROWH), pl.ds(PAD + ROWH + rows, ROWH), pl.ds(PAD + ROWH, rows)
    right_halo, left_halo = pl.ds(width, COLH), pl.ds(width + COLH, COLH)
    halo_plan = (
        ((below_dev, me), (end_rows, all_cols), (top_halo, all_cols)),
        ((above_dev, me), (top_rows, all_cols), (bot_halo, all_cols)),
        ((swath, left_dev), (all_rows, first_cols), (mid_rows, right_halo)),
        ((swath, right_dev), (all_rows, end_cols), (mid_rows, left_halo)),
        ((below_dev, left_dev), (end_rows, first_cols), (top_halo, right_halo)),
        ((below_dev, right_dev), (end_rows, end_cols), (top_halo, left_halo)),
        ((above_dev, left_dev), (top_rows, first_cols), (bot_halo, right_halo)),
        ((above_dev, right_dev), (top_rows, end_cols), (bot_halo, left_halo)),
    )

    def halo_copy(n):
        target, src, dst = halo_plan[n]
        rows_src, cols_src = src
        return pltpu.make_async_remote_copy(
            src_ref=s0.at[pl.ds(PAD + ROWH + rows_src.start, rows_src.size), cols_src],
            dst_ref=s0.at[dst],
            send_sem=halo_send.at[n],
            recv_sem=halo_recv.at[n],
            device_id=target,
            device_id_type=mesh_ids,
        )

    load = pltpu.make_async_copy(raw_t, tile_t, load_sem.at[0])
    load.start()
    barrier = pltpu.get_barrier_semaphore()
    for target, _, _ in halo_plan:
        pl.semaphore_signal(barrier, inc=1, device_id=target, device_id_type=mesh_ids)
    pl.semaphore_wait(barrier, len(halo_plan))
    load.wait()

    def flip(i, j):
        block = tile_t[pl.ds(j * 128, 128), pl.ds(pl.multiple_of(i * 128, 128), 128)]
        s0[pl.ds(pl.multiple_of(PAD + ROWH + i * 128, 8), 128), pl.ds(j * 128, 128)] = block.T

    row_bands, col_bands = rows // 128, width // 128
    for i in range(row_bands):
        for j in range(col_bands):
            if i in (0, row_bands - 1) or j in (0, col_bands - 1):
                flip(i, j)
    for n in range(len(halo_plan)):
        halo_copy(n).start()

    def flip_inner(i, carry):
        for j in range(1, col_bands - 1):
            flip(i, j)
        return carry


    zeros_pad = jnp.zeros((PAD, ext_w), jnp.float32)
    for buf in (s0, s1, s2, s3):
        buf[pl.ds(0, PAD), :] = zeros_pad
        buf[pl.ds(PAD + ext_r, PAD), :] = zeros_pad
    fv_last[...] = jnp.zeros(fv_last.shape, jnp.float32)
    for n in range(len(halo_plan)):
        halo_copy(n).wait_recv()
    for n in range(len(halo_plan)):
        halo_copy(n).wait_send()

    lane = lax.broadcasted_iota(jnp.int32, (BLK, ext_w), 1)
    gcol = col_base + lane - jnp.where(lane >= width + COLH, ext_w, 0)
    col_edge = (gcol >= 0) & (gcol <= band_cols - 2)
    sub = lax.broadcasted_iota(jnp.int32, (BLK, ext_w), 0)
    stages = (s0, s1, s2, s3, s0)

    def step_block(k, b):
        src, dst = stages[k], stages[k + 1]
        r0 = pl.multiple_of(PAD + b * BLK, BLK)
        pair = src[pl.ds(r0, 2 * BLK), :]
        here = pair[:BLK]
        below = pltpu.roll(pair, 2 * BLK - 1, 0)[:BLK]
        grow = row_base + b * BLK + sub
        row_edge = (grow >= 0) & (grow <= band_rows - 2)
        down = jnp.where(row_edge, conduct_flux(below - here), 0.0)
        above = pltpu.roll(fv_last[k], 1, 0)[0:1]
        up = jnp.where(sub == 0, above, pltpu.roll(down, 1, 0))
        fv_last[k] = down[BLK - 8:]
        right = pltpu.roll(here, ext_w - 1, 1)
        across = jnp.where(col_edge, conduct_flux(right - here), 0.0)
        left = pltpu.roll(across, 1, 1)
        dst[pl.ds(r0, BLK), :] = here + step_rate * ((down - up) + (across - left))

    roll_by = lax.rem(ext_w - shift_c, ext_w)
    gcol_a = col_base + shift_c + lax.broadcasted_iota(jnp.int32, (BLK, width), 1)
    col_in = (gcol_a >= 0) & (gcol_a < band_cols)
    sub_a = lax.broadcasted_iota(jnp.int32, (BLK, width), 0)
    row_roll = 2 * BLK - (ROWH + shift_r)

    def send(a, side_index):
        rows_a = pl.ds(pl.multiple_of(a * BLK, BLK), BLK)
        target = from_left if side_index == 0 else from_right
        return pltpu.make_async_remote_copy(
            src_ref=held.at[rows_a],
            dst_ref=target.at[rows_a],
            send_sem=send_sem.at[side_index, a],
            recv_sem=recv_sem.at[side_index, a],
            device_id=(swath, right_dev if side_index == 0 else left_dev),
            device_id_type=mesh_ids,
        )

    def emit(a):
        r0 = pl.multiple_of(PAD + a * BLK, BLK)
        block = s0[pl.ds(r0, 2 * BLK), :]
        block = pltpu.roll(block, row_roll, 0)[:BLK]
        block = pltpu.roll(block, roll_by, 1)[:, :width]
        grow = prm[0] + shift_r + a * BLK + sub_a
        keep = col_in & (grow >= 0) & (grow < band_rows)
        held[pl.ds(pl.multiple_of(a * BLK, BLK), BLK), :] = jnp.where(keep, block, 0.0)
        send(a, 0).start()
        send(a, 1).start()

    def wave(i, carry):
        @pl.when((i % 2 == 1) & (i <= 2 * (row_bands - 2) - 1))
        def _():
            flip_inner((i + 1) // 2, 0)

        for k in range(STEPS):
            b = i - k

            @pl.when((b >= 0) & (b < blocks))
            def _():
                step_block(k, b)

        a = i - STEPS

        @pl.when((a >= 0) & (a < out_blocks))
        def _():
            emit(a)

        return carry

    lax.fori_loop(0, blocks + STEPS, wave, 0)
    diff_copy = pltpu.make_async_copy(s0.at[mid_rows, all_cols], diff_out, out_sem.at[0])
    diff_copy.start()

    def finish(a, carry):
        for side_index in (0, 1):
            send(a, side_index).wait_recv()
        for side_index in (0, 1):
            send(a, side_index).wait_send()
        rows_a = pl.ds(pl.multiple_of(a * BLK, BLK), BLK)
        defect_buf[rows_a, :] = three_die(held[rows_a, :], from_left[rows_a, :], from_right[rows_a, :])
        pltpu.make_async_copy(defect_buf.at[rows_a], defect_out.at[rows_a], out_sem.at[1]).start()
        return carry

    lax.fori_loop(0, out_blocks, finish, 0)
    defect_copy = pltpu.make_async_copy(defect_buf, defect_out, out_sem.at[1])
    diff_copy.wait()
    defect_copy.wait()


def inspect(prm, raw_t, band_rows, band_cols):
    width, rows = raw_t.shape
    ext_w = width + 2 * COLH
    out_blocks = rows // BLK
    buf = pltpu.VMEM((rows + 2 * ROWH + 2 * PAD, ext_w), jnp.float32)
    die = pltpu.VMEM((rows, width), jnp.float32)
    return pl.pallas_call(
        functools.partial(inspect_kernel, band_rows, band_cols),
        out_shape=(jax.ShapeDtypeStruct((rows, width), jnp.float32),) * 2,
        in_specs=[pl.BlockSpec(memory_space=pltpu.SMEM), pl.BlockSpec(memory_space=pl.ANY)],
        out_specs=(pl.BlockSpec(memory_space=pl.ANY), pl.BlockSpec(memory_space=pl.ANY)),
        scratch_shapes=[
            buf, buf, buf, buf,
            pltpu.VMEM((STEPS, 8, ext_w), jnp.float32),
            die, die, die,
            pltpu.SemaphoreType.DMA((2, out_blocks)),
            pltpu.SemaphoreType.DMA((2, out_blocks)),
            pltpu.SemaphoreType.DMA((8,)),
            pltpu.SemaphoreType.DMA((8,)),
            pltpu.SemaphoreType.DMA((1,)),
            die,
            pltpu.SemaphoreType.DMA((2,)),
            die,
        ],
        compiler_params=pltpu.CompilerParams(
            vmem_limit_bytes=64000 * 1024, collective_id=0, has_side_effects=True
        ),
        cost_estimate=pl.CostEstimate(
            flops=STEPS * 40 * (rows + 2 * ROWH) * ext_w, bytes_accessed=4 * 3 * rows * width, transcendentals=0
        ),
    )(prm, raw_t)


def local(raw_band, section_offsets):
    col_count = lax.axis_size("col")
    swath_count = lax.axis_size("swath")
    row_total, die_width = raw_band.shape
    raw_t = lax.all_to_all(raw_band.T, "col", split_axis=0, concat_axis=0, tiled=True)
    swath_index = lax.axis_index("swath")
    col_index = lax.axis_index("col")
    band_rows = swath_count * row_total
    band_cols = col_count * die_width
    die_ids = lax.broadcasted_iota(jnp.int32, section_offsets.shape, 0)
    own_shift = jnp.sum(jnp.where(die_ids == col_index, section_offsets, 0), axis=0)
    prm = jnp.stack(
        [swath_index * row_total, col_index * die_width, own_shift[0], own_shift[1]]
        + [jnp.int32(0)] * 4
    ).astype(jnp.int32)
    return inspect(prm, raw_t, band_rows, band_cols)


def solution(mesh):
    in_specs = (P("swath", "col"), P())
    out_specs = (P("swath", "col"), P("swath", "col"))
    return jax.shard_map(local, mesh=mesh, in_specs=in_specs, out_specs=out_specs, check_vma=False)
```
